32 devices in a mesh: req: 16 (over z, y, x), mlp: 2 (over core).
Axes of the slice: x: 2, y: 2, z: 4, core: 2. Of those that a mesh axis runs over, the one named last changes fastest.
Arguments:
- queries: bfloat16 [16, 256, 1536], P('req'), may hold values from -90 to 90
- cached_key_slots: bfloat16 [16, 8192, 512], P('req', 'mlp'), may hold values from -5 to 5
- cached_value_slots: bfloat16 [16, 8192, 512], P('req', 'mlp'), may hold values from -6 to 6
- new_token_keys: bfloat16 [16, 256, 512], P('req', 'mlp'), may hold values from -5.05 to 5.05
- new_token_values: bfloat16 [16, 256, 512], P('req', 'mlp'), may hold values from -6 to 6
- cache_len: int32 [16], replicated, may hold values from 1 to 8192, 65536 in all
- placing: int32 [16], replicated, may hold values from 0 to 15, each once
- w_gate: bfloat16 [1536, 12288], P('req', 'mlp'), may hold values from -0.15625 to 0.15625
- w_up: bfloat16 [1536, 12288], P('req', 'mlp'), may hold values from -0.15625 to 0.15625
- w_down: bfloat16 [12288, 1536], P('mlp', 'req'), may hold values from -0.0546875 to 0.0546875
Outputs:
- mixed: bfloat16 [16, 256, 1536], P('req', 'mlp')
The draws below stay inside these ranges and needn't reach their ends.
All inputs are finite; a program needn't handle non-finite values.
Results may differ from the reference program's by a relative error of at most 0.019.
Values may be sent and summed in bfloat16 or wider, within the bound.
A program may use at most 192 MiB of HBM per device.

```python
import math
import jax
import jax.numpy as jnp
import numpy as np
from jax import lax

HEAD_SIZE = 256
QUERY_HEADS = 6
KEY_VALUE_HEADS = 2
D = 1536
FF = 12288
NEW_TOKENS = 256
CACHE_SLOTS = 8192
REQUEST_COUNT = 16


def leading_keys(key):
    return jnp.clip(jax.random.normal(jax.random.fold_in(key, 11), (REQUEST_COUNT, KEY_VALUE_HEADS * HEAD_SIZE), jnp.float32), -5.0, 5.0)


def draw_cached_key_slots(key, part):
    remaining_items = jnp.clip(jax.random.normal(jax.random.fold_in(key, 12), (REQUEST_COUNT, CACHE_SLOTS, KEY_VALUE_HEADS * HEAD_SIZE), jnp.float32), -5.0, 5.0)
    position = jnp.arange(CACHE_SLOTS)[None, :, None]
    remaining_items = jnp.where(position == 0, leading_keys(key)[:, None, :], remaining_items)
    return remaining_items.astype(jnp.bfloat16)


def draw_queries(key, part):
    start_offset = jnp.clip(jax.random.normal(jax.random.fold_in(key, 13), (REQUEST_COUNT, NEW_TOKENS, QUERY_HEADS * HEAD_SIZE), jnp.float32), -5.0, 5.0)
    return start_offset.astype(jnp.bfloat16)


def draw_new_token_keys(key, part):
    start_offset = jnp.clip(jax.random.normal(jax.random.fold_in(key, 14), (REQUEST_COUNT, NEW_TOKENS, KEY_VALUE_HEADS * HEAD_SIZE), jnp.float32), -5.0, 5.0)
    return start_offset.astype(jnp.bfloat16)


def steps_of(rng, dims, shards, least, high):
    loudness, own = 1.0, jax.random.fold_in(rng, 6)
    for dim, shards_of in shards:
        steps = jnp.exp(jax.random.uniform(jax.random.fold_in(own, dim), (shards_of,), jnp.float32, least / len(shards), high / len(shards)))
        loudness = loudness * jnp.repeat(steps, dims[dim] // shards_of).reshape([-1 if axis == dim else 1 for axis in range(len(dims))])
    return loudness


def profile(amount, total, limit, skew):
    portions = [(1 << 20) // math.isqrt(standing ** skew) + 1 for standing in range(2, amount + 1)]
    spare, given = total - limit - (amount - 1), [1] * (amount - 1)
    while spare > 0:
        candidates = [i for i in range(amount - 1) if given[i] < limit]
        mass, left = sum([portions[i] for i in candidates]), spare
        for i in candidates:
            extra = min(limit - given[i], max(1, left * portions[i] // mass), spare)
            given[i] = given[i] + extra
            spare = spare - extra
    return np.array([limit] + given)


def uneven(own_key, count, total, limit, skew):
    if count == 2:
        one = jax.random.randint(own_key, (), max(1, total - limit), min(limit, total - 1) + 1)
        return jnp.stack([one, total - one])
    sizes = jnp.asarray(profile(count, total, limit, skew), jnp.int32)
    twos = (count - 1) // 2
    source_of, sink = sizes[1:1 + 2 * twos:2], sizes[2:2 + 2 * twos:2]
    room = jnp.minimum(source_of - 1, limit - sink)
    passed = jax.random.randint(jax.random.fold_in(own_key, 1), (twos,), 0, 1 << 20) % (room + 1)
    sizes = sizes.at[1:1 + 2 * twos:2].set(source_of - passed).at[2:2 + 2 * twos:2].set(sink + passed)
    return sizes[jax.random.permutation(jax.random.fold_in(own_key, 2), count)]


def scatter_about(rng, shape, scale, most, cuts=(), kind=jnp.bfloat16):
    values = scale * jax.random.normal(rng, shape, jnp.float32)
    if cuts:
        values = values * steps_of(rng, shape, cuts, -0.22, 0.18)
    return jnp.clip(values, -most, most).astype(kind)


def setup_inputs(seed: int = 0) -> dict:
    key_of = jax.random.split(jax.random.key(seed), 11)
    queries = draw_queries(jax.random.fold_in(key_of[10], 71), 0)
    cached_key_slots = draw_cached_key_slots(jax.random.fold_in(key_of[10], 71), 0)
    cached_value_slots = scatter_about(key_of[2], (REQUEST_COUNT, CACHE_SLOTS, KEY_VALUE_HEADS * HEAD_SIZE), 1.0, 6.0, ((0, 16), (1, 2)))
    new_token_keys = draw_new_token_keys(jax.random.fold_in(key_of[10], 71), 0)
    new_token_values = scatter_about(key_of[4], (REQUEST_COUNT, NEW_TOKENS, KEY_VALUE_HEADS * HEAD_SIZE), 1.0, 6.0, ((0, 16), (1, 2)))
    cache_len = uneven(key_of[5], REQUEST_COUNT, REQUEST_COUNT * CACHE_SLOTS // 2, CACHE_SLOTS, 2).astype(jnp.int32)
    placing = jax.random.permutation(key_of[6], REQUEST_COUNT).astype(jnp.int32)
    w_gate = scatter_about(key_of[7], (D, FF), D ** -0.5, 0.15625, ((0, 16), (1, 2)))
    w_up = scatter_about(key_of[8], (D, FF), D ** -0.5, 0.15625, ((0, 16), (1, 2)))
    w_down = scatter_about(key_of[9], (FF, D), FF ** -0.5, 0.0546875, ((0, 2), (1, 16)))
    return dict(queries=queries, cached_key_slots=cached_key_slots, cached_value_slots=cached_value_slots, new_token_keys=new_token_keys, new_token_values=new_token_values, cache_len=cache_len, placing=placing, w_gate=w_gate, w_up=w_up, w_down=w_down)


score_scale = 0.0625
negative = -1e+30

def attend_slot(query_token_rows, joined_keys, joined_values, new_key_rows, new_value_rows, live_len):
    query_group_width = QUERY_HEADS // KEY_VALUE_HEADS
    query_head_rows = query_token_rows.astype(jnp.float32).reshape(NEW_TOKENS, KEY_VALUE_HEADS, query_group_width, HEAD_SIZE)
    key_head_rows = joined_keys.astype(jnp.float32).reshape(CACHE_SLOTS, KEY_VALUE_HEADS, HEAD_SIZE)
    value_head_rows = joined_values.astype(jnp.float32).reshape(CACHE_SLOTS, KEY_VALUE_HEADS, HEAD_SIZE)
    new_token_keys = new_key_rows.astype(jnp.float32).reshape(NEW_TOKENS, KEY_VALUE_HEADS, HEAD_SIZE)
    new_token_values = new_value_rows.astype(jnp.float32).reshape(NEW_TOKENS, KEY_VALUE_HEADS, HEAD_SIZE)
    scores_old = jnp.einsum('ngrd,cgd->grnc', query_head_rows, key_head_rows) * score_scale
    cache_live = jnp.arange(CACHE_SLOTS, dtype=jnp.int32) < live_len
    scores_old = jnp.where(cache_live[None, None, None, :], scores_old, negative)
    scores_new = jnp.einsum('ngrd,mgd->grnm', query_head_rows, new_token_keys) * score_scale
    causal = jnp.arange(NEW_TOKENS, dtype=jnp.int32)[None, :] <= jnp.arange(NEW_TOKENS, dtype=jnp.int32)[:, None]
    scores_new = jnp.where(causal[None, None], scores_new, negative)
    row_top = jnp.maximum(scores_old.max(-1), scores_new.max(-1))
    expo_old = jnp.exp(scores_old - row_top[..., None])
    expo_new = jnp.exp(scores_new - row_top[..., None])
    denom = expo_old.sum(-1) + expo_new.sum(-1)
    probs_old = lax.optimization_barrier(expo_old.astype(jnp.bfloat16)).astype(jnp.float32)
    probs_new = lax.optimization_barrier(expo_new.astype(jnp.bfloat16)).astype(jnp.float32)
    weighted = jnp.einsum('grnc,cgd->ngrd', probs_old, value_head_rows)
    weighted = weighted + jnp.einsum('grnm,mgd->ngrd', probs_new, new_token_values)
    attended = weighted / jnp.transpose(denom, (2, 0, 1))[..., None]
    return attended.reshape(NEW_TOKENS, QUERY_HEADS * HEAD_SIZE).astype(jnp.bfloat16)

def reference(queries, cached_key_slots, cached_value_slots, new_token_keys, new_token_values, cache_len, placing, w_gate, w_up, w_down):
    live = cache_len[placing].astype(jnp.int32)

    def one_slot(items):
        query_token_rows, joined_keys, joined_values, new_key_rows, new_value_rows, live_len = items
        attended = attend_slot(query_token_rows, joined_keys, joined_values, new_key_rows, new_value_rows, live_len)
        wide = attended.astype(jnp.float32)
        normed = (wide * lax.rsqrt(lax.optimization_barrier(jnp.mean(wide * wide, axis=-1, keepdims=True)) + 1e-06)).astype(jnp.bfloat16)
        gate = jnp.dot(normed, w_gate, preferred_element_type=jnp.float32)
        upper = jnp.dot(normed, w_up, preferred_element_type=jnp.float32)
        hidden = (jax.nn.silu(gate) * upper).astype(jnp.bfloat16)
        down = jnp.dot(hidden, w_down, preferred_element_type=jnp.float32)
        return (wide + down).astype(jnp.bfloat16)
    return lax.map(one_slot, (queries, cached_key_slots, cached_value_slots, new_token_keys, new_token_values, live))
```

```python
import functools

import jax
import jax.numpy as jnp
from jax import lax
from jax.experimental import pallas as pl
from jax.experimental.pallas import tpu as pltpu
from jax.sharding import PartitionSpec as P

HEAD_SIZE = 256
QUERY_HEADS = 6
KEY_VALUE_HEADS = 2


score_scale = 0.0625
negative = -1e30


def lookup(table, index):
    positions = jnp.arange(table.shape[0], dtype=jnp.int32)
    return jnp.sum(jnp.where(positions == index, table, 0))


def rms_rows(attended):
    wide = attended.astype(jnp.float32)
    return (wide * lax.rsqrt(jnp.mean(wide * wide, axis=-1, keepdims=True) + 1e-06)).astype(
        jnp.bfloat16
    )


def wide_body(
    queries,
    cached_key_slots,
    cached_value_slots,
    new_token_keys,
    new_token_values,
    cache_len,
    placing,
    w_gate,
    w_up,
    w_down,
):
    slot_index = lax.axis_index("req")
    mlp_index = lax.axis_index("mlp")
    mlp_count = lax.axis_size("mlp")
    token_inputs = queries.shape[1]
    request_cache = cached_key_slots.shape[1]
    request_new_tokens = new_token_keys.shape[1]
    query_group_width = QUERY_HEADS // KEY_VALUE_HEADS
    row_count = token_inputs // mlp_count
    request = lookup(placing, slot_index)
    live_len = lookup(cache_len, request)
    query_head_rows = queries[0].reshape(
        token_inputs, KEY_VALUE_HEADS, query_group_width, HEAD_SIZE
    )
    request_keys = cached_key_slots[0].reshape(request_cache, KEY_VALUE_HEADS, HEAD_SIZE)
    request_values = cached_value_slots[0].reshape(request_cache, KEY_VALUE_HEADS, HEAD_SIZE)
    new_key_rows = new_token_keys[0].reshape(request_new_tokens, KEY_VALUE_HEADS, HEAD_SIZE)
    new_value_rows = new_token_values[0].reshape(request_new_tokens, KEY_VALUE_HEADS, HEAD_SIZE)
    cache_pos = mlp_index * request_cache + jnp.arange(request_cache, dtype=jnp.int32)
    cache_live = cache_pos < live_len
    scores_old = (
        jnp.einsum(
            "ngrd,cgd->grnc", query_head_rows, request_keys, preferred_element_type=jnp.float32
        )
        * score_scale
    )
    scores_old = jnp.where(cache_live[None, None, None, :], scores_old, negative)
    fresh_pos = mlp_index * request_new_tokens + jnp.arange(request_new_tokens, dtype=jnp.int32)
    causal = fresh_pos[None, :] <= jnp.arange(token_inputs, dtype=jnp.int32)[:, None]
    scores_new = (
        jnp.einsum(
            "ngrd,mgd->grnm", query_head_rows, new_key_rows, preferred_element_type=jnp.float32
        )
        * score_scale
    )
    scores_new = jnp.where(causal[None, None], scores_new, negative)
    local_top = jnp.maximum(scores_old.max(-1), scores_new.max(-1))
    row_top = lax.pmax(local_top, "mlp")
    expo_old = jnp.exp(scores_old - row_top[..., None])
    expo_new = jnp.exp(scores_new - row_top[..., None])
    denom_local = expo_old.sum(-1) + expo_new.sum(-1)
    probs_old = expo_old.astype(jnp.bfloat16)
    probs_new = expo_new.astype(jnp.bfloat16)
    weighted = jnp.einsum(
        "grnc,cgd->ngrd", probs_old, request_values, preferred_element_type=jnp.float32
    )
    weighted = weighted + jnp.einsum(
        "grnm,mgd->ngrd", probs_new, new_value_rows, preferred_element_type=jnp.float32
    )
    weighted, denom = lax.psum((weighted, denom_local), "mlp")
    attended = (
        (weighted / jnp.transpose(denom, (2, 0, 1))[..., None])
        .reshape(token_inputs, QUERY_HEADS * HEAD_SIZE)
        .astype(jnp.bfloat16)
    )
    normed = rms_rows(attended)
    own_attended = lax.dynamic_slice_in_dim(attended, mlp_index * row_count, row_count, 0)
    gate_sum = jnp.dot(
        normed,
        lax.all_gather(w_gate, "req", axis=0, tiled=True),
        preferred_element_type=jnp.float32,
    )
    upper_sum = jnp.dot(
        normed, lax.all_gather(w_up, "req", axis=0, tiled=True), preferred_element_type=jnp.float32
    )
    hidden = (jax.nn.silu(gate_sum) * upper_sum).astype(jnp.bfloat16)
    partial_down = jnp.dot(
        hidden,
        lax.all_gather(w_down, "req", axis=1, tiled=True),
        preferred_element_type=jnp.float32,
    )
    own_rows = lax.psum_scatter(
        partial_down.astype(jnp.bfloat16), "mlp", scatter_dimension=0, tiled=True
    ).astype(jnp.float32)
    residual = own_attended.astype(jnp.float32)
    return (residual + own_rows).astype(jnp.bfloat16)[None]


CHUNKS = 3
KEY_BLOCK = 512
CACHE_PARTS = 4
FAR_WINDOW = 2


def other(index, mask, bits):
    flipped = 0
    for b in range(bits):
        flipped = flipped + ((index // (1 << b) + mask // (1 << b)) % 2) * (1 << b)
    return flipped


def settle(ref, sem):
    pltpu.make_async_copy(ref, ref, sem).wait()


def window_kernel(
    cache_len_ref,
    placing_ref,
    queries_ref,
    keys_ref,
    values_ref,
    new_keys_ref,
    new_values_ref,
    gate_ref,
    upper_ref,
    down_ref,
    out_ref,
    weights,
    keys,
    values,
    queries,
    new_keys,
    new_values,
    weighted,
    top,
    denom,
    share_out,
    share_in,
    own_attended,
    normed,
    total,
    pair_out,
    pair_in,
    chain_out,
    chain_in,
    plane_send,
    plane_recv,
    across_send,
    across_recv,
    core_send,
    core_recv,
    own_sem,
    load_sem,
    cache_sem,
    share_send,
    share_recv,
    token_send,
    token_recv,
    pair_send,
    pair_recv,
    chain_send,
    chain_recv,
):
    slot = lax.axis_index("req")
    core = lax.axis_index("mlp")
    x, p = slot % 2, slot // 2
    y, z = p % 2, p // 2
    beside = p + 1 - 2 * y
    strip = gate_ref.shape[0]
    width = out_ref.shape[1]
    rows = out_ref.shape[0]
    units = gate_ref.shape[1] // 8
    piece = units // CHUNKS
    chunk = 2 * piece
    group = QUERY_HEADS // KEY_VALUE_HEADS
    tokens = 2 * rows

    def at(place, column):
        return {"req": place * 2 + column, "mlp": core}

    def in_plane(place):
        return at(place, x)

    across = at(p, 1 - x)
    twin = {"req": slot, "mlp": 1 - core}

    def push(source, target, send_sem, recv_sem, device):
        pltpu.make_async_remote_copy(
            src_ref=source,
            dst_ref=target,
            send_sem=send_sem,
            recv_sem=recv_sem,
            device_id=device,
            device_id_type=pl.DeviceIdType.MESH,
        ).start()

    barrier = pltpu.get_barrier_semaphore()
    peers = [in_plane(other(p, k, 3)) for k in range(1, 8)] + [across, twin]
    for peer in peers:
        pl.semaphore_signal(barrier, inc=1, device_id=peer, device_id_type=pl.DeviceIdType.MESH)
    pl.semaphore_wait(barrier, len(peers))

    sources = (gate_ref, upper_ref, down_ref)

    def strip_rows(place, column):
        return pl.ds(pl.multiple_of((place * 2 + column) * strip, 16), strip)

    def piece_columns(j, half):
        return pl.ds(pl.multiple_of(j * chunk + half * piece, 128), piece)

    def source_columns(j, place):
        return pl.ds(pl.multiple_of(place * units + j * piece, 128), piece)

    def issue(j, k):
        place = other(p, k, 3)
        for m in range(3):
            push(
                sources[m].at[:, source_columns(j, place)],
                weights.at[m, strip_rows(p, x), piece_columns(j, core)],
                plane_send.at[j],
                plane_recv.at[j, k],
                in_plane(place),
            )

    def issue_own(j):
        for m in range(3):
            source = sources[m].at[:, source_columns(j, p)]
            target = weights.at[m, strip_rows(p, x), piece_columns(j, core)]
            pltpu.make_async_copy(source, target, own_sem).start()
            push(source, target, across_send, across_recv.at[j, 0], across)
            push(source, target, core_send, core_recv.at[j], twin)

    def block_of(j, k, column):
        return weights.at[:, strip_rows(other(p, k, 3), column), piece_columns(j, core)]

    def relay(j, k):
        block = block_of(j, k, x)
        settle(block, plane_recv.at[j, k])
        push(block, block, across_send, across_recv.at[j, k], across)
        push(block, block, core_send, core_recv.at[j], twin)

    def relay_across(j, k):
        block = block_of(j, k, 1 - x)
        settle(block, across_recv.at[j, k])
        push(block, block, core_send, core_recv.at[j], twin)

    def chunk_done(j):
        settle(weights.at[:, :, piece_columns(j, 1 - core)], core_recv.at[j])

    far = [(j, k) for j in range(CHUNKS) for k in (4, 5, 6, 7)]
    near = [(j, k) for j in range(CHUNKS) for k in (1, 2, 3)]

    def far_step(f):
        relay(*far[f])
        if f + FAR_WINDOW < len(far):
            issue(*far[f + FAR_WINDOW])

    for f in range(FAR_WINDOW):
        issue(*far[f])

    part = keys_ref.shape[0] // CACHE_PARTS
    pltpu.make_async_copy(queries_ref, queries, load_sem.at[0]).start()
    pltpu.make_async_copy(new_keys_ref, new_keys, load_sem.at[1]).start()
    pltpu.make_async_copy(new_values_ref, new_values, load_sem.at[2]).start()
    for n in range(CACHE_PARTS):
        span = pl.ds(n * part, part)
        pltpu.make_async_copy(keys_ref.at[span], keys.at[span], cache_sem.at[0, n]).start()
        pltpu.make_async_copy(values_ref.at[span], values.at[span], cache_sem.at[1, n]).start()
    for j in range(CHUNKS):
        issue_own(j)
    for pair in near:
        issue(*pair)

    live_len = cache_len_ref[placing_ref[slot]]
    settle(queries, load_sem.at[0])
    settle(new_keys, load_sem.at[1])
    settle(new_values, load_sem.at[2])
    queries[...] = queries[...] * jnp.bfloat16(score_scale)

    def against(a, b):
        return lax.dot_general(
            a, b, (((1,), (1,)), ((), ())), preferred_element_type=jnp.float32
        )

    def lanes(h, size):
        return pl.ds(pl.multiple_of(h * size, 128), size)

    def spread(narrow, size):
        return jnp.concatenate([narrow] * (size // 128), axis=1)

    def folded(wide_rows):
        parts = [wide_rows[:, n : n + 128] for n in range(0, wide_rows.shape[1], 128)]
        while len(parts) > 1:
            parts = [parts[n] + parts[n + 1] for n in range(0, len(parts), 2)]
        return parts[0]

    fresh_pos = core * rows + lax.broadcasted_iota(jnp.int32, (tokens, rows), 1)
    causal = fresh_pos <= lax.broadcasted_iota(jnp.int32, (tokens, rows), 0)
    for h in range(QUERY_HEADS):
        g = h // group
        head = queries[:, h * HEAD_SIZE : (h + 1) * HEAD_SIZE]
        scores = against(head, new_keys[:, g * HEAD_SIZE : (g + 1) * HEAD_SIZE])
        scores = jnp.where(causal, scores, negative)
        row_top = jnp.broadcast_to(jnp.max(scores, axis=1, keepdims=True), (tokens, 128))
        expo = jnp.exp(scores - spread(row_top, rows))
        top[h] = row_top
        denom[h] = folded(expo)
        weighted[h] = jnp.dot(
            expo.astype(jnp.bfloat16),
            new_values[:, g * HEAD_SIZE : (g + 1) * HEAD_SIZE],
            preferred_element_type=jnp.float32,
        )

    def attend_block(g, start):
        span = pl.ds(pl.multiple_of(start, KEY_BLOCK), KEY_BLOCK)
        block_keys = keys[span, lanes(g, HEAD_SIZE)]
        block_values = values[span, lanes(g, HEAD_SIZE)]
        cache_pos = core * keys.shape[0] + start
        live = cache_pos + lax.broadcasted_iota(jnp.int32, (1, KEY_BLOCK), 1) < live_len
        for n in range(group):
            h = g * group + n
            scores = against(queries[:, lanes(h, HEAD_SIZE)], block_keys)
            scores = jnp.where(live, scores, negative)
            old_top = top[h]
            row_top = jnp.maximum(old_top, jnp.max(scores, axis=1, keepdims=True))
            fade = jnp.exp(old_top - row_top)
            expo = jnp.exp(scores - spread(row_top, KEY_BLOCK))
            top[h] = row_top
            denom[h] = denom[h] * fade + folded(expo)
            weighted[h] = weighted[h] * spread(fade, HEAD_SIZE) + jnp.dot(
                expo.astype(jnp.bfloat16), block_values, preferred_element_type=jnp.float32
            )

    def share(h):
        away = pl.ds(pl.multiple_of((1 - core) * rows, rows), rows)
        share_out[h, :, :HEAD_SIZE] = weighted[h, away, :]
        share_out[h, :, HEAD_SIZE : HEAD_SIZE + 128] = top[h, away, :]
        share_out[h, :, HEAD_SIZE + 128 :] = denom[h, away, :]
        push(share_out.at[h], share_in.at[h], share_send, share_recv, twin)

    steps = KEY_VALUE_HEADS * CACHE_PARTS
    plan = {s: [] for s in range(steps)}
    for n, pair in enumerate(near):
        plan[min(steps - 1, 2 + n // 2)].append(functools.partial(relay, *pair))
    for n, pair in enumerate([(j, k) for j in range(CHUNKS) for k in range(4)]):
        plan[min(steps - 1, 3 + n // 2)].append(functools.partial(relay_across, *pair))
    for f, s in ((0, 4), (1, 5), (2, 7)):
        plan[s].append(functools.partial(far_step, f))

    def attend_step(s, carry):
        g, n = s // CACHE_PARTS, s % CACHE_PARTS

        @pl.when(s < CACHE_PARTS)
        def _():
            span = pl.ds(pl.multiple_of(n * part, part), part)
            settle(keys.at[span], cache_sem.at[0, n])
            settle(values.at[span], cache_sem.at[1, n])

        def inner(i, c):
            attend_block(g, n * part + i * KEY_BLOCK)
            return c

        lax.fori_loop(0, part // KEY_BLOCK, inner, 0)

        @pl.when(n == CACHE_PARTS - 1)
        def _():
            for i in range(group):
                share(g * group + i)

        for step, events in plan.items():
            if events:

                @pl.when(s == step)
                def _():
                    for event in events:
                        event()

        return carry

    lax.fori_loop(0, steps, attend_step, 0)

    settle(share_in, share_recv)
    mine = pl.ds(pl.multiple_of(core * rows, rows), rows)
    squares = jnp.zeros((rows, 128), jnp.float32)
    for h in range(QUERY_HEADS):
        own_top, peer_top = top[h, mine, :], share_in[h, :, HEAD_SIZE : HEAD_SIZE + 128]
        row_top = jnp.maximum(own_top, peer_top)
        own_scale, peer_scale = jnp.exp(own_top - row_top), jnp.exp(peer_top - row_top)
        lane_sums = denom[h, mine, :] * own_scale + share_in[h, :, HEAD_SIZE + 128 :] * peer_scale
        head = weighted[h, mine, :] * spread(own_scale, HEAD_SIZE)
        head = head + share_in[h, :, :HEAD_SIZE] * spread(peer_scale, HEAD_SIZE)
        head = (head / jnp.sum(lane_sums, axis=1, keepdims=True)).astype(jnp.bfloat16)
        own_attended[:, h * HEAD_SIZE : (h + 1) * HEAD_SIZE] = head
        wide = head.astype(jnp.float32)
        squares = squares + folded(wide * wide)
    scale = lax.rsqrt(jnp.sum(squares, axis=1, keepdims=True) / width + 1e-06)

    def token_rows(place, count=1):
        return pl.ds(pl.multiple_of(place * rows, rows), count * rows)

    normed[token_rows(p), :] = (own_attended[...].astype(jnp.float32) * scale).astype(jnp.bfloat16)

    def pass_on(place, way, d, device):
        block = normed.at[token_rows(place)]
        push(block, block, token_send.at[way, d], token_recv.at[place], device)

    def sent(place, way, d):
        settle(normed.at[token_rows(place)], token_send.at[way, d])

    def spread_tokens(d):
        below, above = p - 2 * d, p + 2 * d
        if d == 0:
            pl.when(z < 3)(lambda: pass_on(p, 1, 0, in_plane(p + 2)))
            pl.when(z > 0)(lambda: pass_on(p, 2, 0, in_plane(p - 2)))
            pass_on(p, 0, 0, in_plane(beside))
            return

        @pl.when(z >= d)
        def _():
            settle(normed.at[token_rows(below)], token_recv.at[below])
            pl.when(z < 3)(lambda: pass_on(below, 1, d, in_plane(p + 2)))
            pass_on(below, 0, d, in_plane(beside))

        @pl.when(z + d <= 3)
        def _():
            settle(normed.at[token_rows(above)], token_recv.at[above])
            pl.when(z > 0)(lambda: pass_on(above, 2, d, in_plane(p - 2)))
            pass_on(above, 0, 3 + d, in_plane(beside))

    def tokens_sent():
        sent(p, 0, 0)
        pl.when(z < 3)(lambda: sent(p, 1, 0))
        pl.when(z > 0)(lambda: sent(p, 2, 0))
        for d in range(1, 4):
            below, above = p - 2 * d, p + 2 * d
            pl.when(z >= d)(functools.partial(sent, below, 0, d))
            pl.when((z >= d) & (z < 3))(functools.partial(sent, below, 1, d))
            pl.when(z + d <= 3)(functools.partial(sent, above, 0, 3 + d))
            pl.when((z + d <= 3) & (z > 0))(functools.partial(sent, above, 2, d))

    def tokens_here():
        for plane in range(4):
            place = plane * 2 + 1 - y
            settle(normed.at[token_rows(place)], token_recv.at[place])

    def mix(j, span):
        columns = pl.ds(j * chunk, chunk)
        inputs = normed[span, :]
        gate_sum = jnp.dot(inputs, weights[0, :, columns], preferred_element_type=jnp.float32)
        upper_sum = jnp.dot(inputs, weights[1, :, columns], preferred_element_type=jnp.float32)
        hidden = (gate_sum / (1.0 + jnp.exp(-gate_sum)) * upper_sum).astype(jnp.bfloat16)
        return against(hidden, weights[2, :, columns])

    half_rows = 4 * rows

    def early(j, half):
        span = pl.ds(half * half_rows, half_rows)
        if j == 0:
            total[span, :] = mix(j, span)
        else:
            total[span, :] += mix(j, span)

    spread_tokens(0)
    far_step(3)
    for f in (0, 1):
        relay_across(*far[f])
    spread_tokens(1)
    far_step(4)
    relay_across(*far[2])
    spread_tokens(2)
    far_step(5)
    relay_across(*far[3])
    spread_tokens(3)
    settle(weights.at[:, pl.ds(0, strip), pl.ds(0, units)], own_sem)
    chunk_done(0)
    far_step(6)
    relay_across(*far[4])
    tokens_here()
    far_step(7)
    relay_across(*far[5])
    early(0, 0)
    far_step(8)
    relay_across(*far[6])
    early(0, 1)
    far_step(9)
    relay_across(*far[7])
    chunk_done(1)
    early(1, 0)
    far_step(10)
    relay_across(*far[8])
    early(1, 1)
    far_step(11)
    for f in (9, 10, 11):
        relay_across(*far[f])
    chunk_done(2)

    upper_half = z // 2
    folded_z = z + upper_half * (3 - 2 * z)

    def plane_of(i):
        base = (3, 2, 1 - folded_z, folded_z)[i]
        return base + upper_half * (3 - 2 * base)

    def last(i):
        plane = plane_of(i)
        span = token_rows(plane * 2, 2)
        total[span, :] += mix(CHUNKS - 1, span)
        pair_out[i] = total[token_rows(plane * 2 + 1 - y), :].astype(jnp.bfloat16)
        push(pair_out.at[i], pair_in.at[i], pair_send.at[i], pair_recv.at[i], in_plane(beside))

    def column_sum(i):
        settle(pair_in.at[i], pair_recv.at[i])
        own = token_rows(plane_of(i) * 2 + y)
        total[own, :] += pair_in[i].astype(jnp.float32)
        return own

    def add_chain(own, way, plane):
        settle(chain_in.at[way, plane], chain_recv.at[way, plane])
        total[own, :] += chain_in[way, plane].astype(jnp.float32)

    def along(i):
        plane = plane_of(i)
        own = column_sum(i)

        def go(way, device, has_more):
            @pl.when(has_more)
            def _():
                add_chain(own, way, plane)

            chain_out[i] = total[own, :].astype(jnp.bfloat16)
            push(
                chain_out.at[i],
                chain_in.at[way, plane],
                chain_send.at[i],
                chain_recv.at[way, plane],
                device,
            )

        pl.when(plane > z)(lambda: go(0, in_plane(p + 2), z > 0))
        pl.when(plane < z)(lambda: go(1, in_plane(p - 2), z < 3))

    last(0)
    last(1)
    along(0)
    last(2)
    last(3)
    along(1)
    along(2)
    own = column_sum(3)
    pl.when(z > 0)(lambda: add_chain(own, 0, z))
    pl.when(z < 3)(lambda: add_chain(own, 1, z))
    out_ref[...] = (own_attended[...].astype(jnp.float32) + total[own, :]).astype(jnp.bfloat16)

    for j in range(CHUNKS):
        settle(weights.at[:, pl.ds(0, 7 * strip), pl.ds(0, piece)], plane_send.at[j])
    settle(weights.at[:, pl.ds(0, 8 * strip), pl.ds(0, units)], across_send)
    settle(weights.at[:, :, pl.ds(0, units)], core_send)
    settle(share_out, share_send)
    tokens_sent()
    for i in range(4):
        settle(pair_out.at[i], pair_send.at[i])
    for i in range(3):
        settle(chain_out.at[i], chain_send.at[i])


def window(
    queries,
    cached_key_slots,
    cached_value_slots,
    new_token_keys,
    new_token_values,
    cache_len,
    placing,
    w_gate,
    w_up,
    w_down,
):
    tokens, width = queries.shape
    rows = tokens // 2
    bf16, f32 = jnp.bfloat16, jnp.float32
    vmem, dma = pltpu.VMEM, pltpu.SemaphoreType.DMA
    hidden_units = w_gate.shape[1] // 4
    scalars = pl.BlockSpec(memory_space=pltpu.SMEM)
    return pl.pallas_call(
        window_kernel,
        out_shape=jax.ShapeDtypeStruct((rows, width), bf16),
        in_specs=[scalars] * 2 + [pl.BlockSpec(memory_space=pl.ANY)] * 8,
        out_specs=pl.BlockSpec(memory_space=pltpu.VMEM),
        scratch_shapes=[
            vmem((3, width, hidden_units), bf16),
            vmem(cached_key_slots.shape, bf16),
            vmem(cached_value_slots.shape, bf16),
            vmem((tokens, width), bf16),
            vmem(new_token_keys.shape, bf16),
            vmem(new_token_values.shape, bf16),
            vmem((QUERY_HEADS, tokens, HEAD_SIZE), f32),
            vmem((QUERY_HEADS, tokens, 128), f32),
            vmem((QUERY_HEADS, tokens, 128), f32),
            vmem((QUERY_HEADS, rows, 2 * HEAD_SIZE), f32),
            vmem((QUERY_HEADS, rows, 2 * HEAD_SIZE), f32),
            vmem((rows, width), bf16),
            vmem((8 * rows, width), bf16),
            vmem((8 * rows, width), f32),
            vmem((4, rows, width), bf16),
            vmem((4, rows, width), bf16),
            vmem((3, rows, width), bf16),
            vmem((2, 4, rows, width), bf16),
            dma((CHUNKS,)),
            dma((CHUNKS, 8)),
            dma,
            dma((CHUNKS, 8)),
            dma,
            dma((CHUNKS,)),
            dma,
            dma((3,)),
            dma((2, CACHE_PARTS)),
            dma,
            dma,
            dma((3, 7)),
            dma((8,)),
            dma((4,)),
            dma((4,)),
            dma((3,)),
            dma((2, 4)),
        ],
        compiler_params=pltpu.CompilerParams(
            collective_id=0, has_side_effects=True, vmem_limit_bytes=60 * 1024 * 1024
        ),
        name="window",
    )(
        cache_len,
        placing,
        queries,
        cached_key_slots,
        cached_value_slots,
        new_token_keys,
        new_token_values,
        w_gate,
        w_up,
        w_down.T,
    )


def body(
    queries,
    cached_key_slots,
    cached_value_slots,
    new_token_keys,
    new_token_values,
    cache_len,
    placing,
    w_gate,
    w_up,
    w_down,
):
    if lax.axis_size("req") != 16 or lax.axis_size("mlp") != 2:
        return wide_body(
            queries,
            cached_key_slots,
            cached_value_slots,
            new_token_keys,
            new_token_values,
            cache_len,
            placing,
            w_gate,
            w_up,
            w_down,
        )
    return window(
        queries[0],
        cached_key_slots[0],
        cached_value_slots[0],
        new_token_keys[0],
        new_token_values[0],
        cache_len,
        placing,
        w_gate,
        w_up,
        w_down,
    )[None]


def solution(mesh):
    in_specs = (
        P("req", None, None),
        P("req", "mlp", None),
        P("req", "mlp", None),
        P("req", "mlp", None),
        P("req", "mlp", None),
        P(),
        P(),
        P("req", "mlp"),
        P("req", "mlp"),
        P("mlp", "req"),
    )
    out_specs = P("req", "mlp", None)
    return jax.shard_map(body, mesh=mesh, in_specs=in_specs, out_specs=out_specs, check_vma=False)
```

```python
import functools

import jax
import jax.numpy as jnp
from jax import lax
from jax.experimental import pallas as pl
from jax.experimental.pallas import tpu as pltpu
from jax.sharding import PartitionSpec as P

HEAD_SIZE = 256
QUERY_HEADS = 6
KEY_VALUE_HEADS = 2


score_scale = 0.0625
negative = -1e30


def lookup(table, index):
    positions = jnp.arange(table.shape[0], dtype=jnp.int32)
    return jnp.sum(jnp.where(positions == index, table, 0))


def rms_rows(attended):
    wide = attended.astype(jnp.float32)
    return (wide * lax.rsqrt(jnp.mean(wide * wide, axis=-1, keepdims=True) + 1e-06)).astype(
        jnp.bfloat16
    )


def wide_body(
    queries,
    cached_key_slots,
    cached_value_slots,
    new_token_keys,
    new_token_values,
    cache_len,
    placing,
    w_gate,
    w_up,
    w_down,
):
    slot_index = lax.axis_index("req")
    mlp_index = lax.axis_index("mlp")
    mlp_count = lax.axis_size("mlp")
    token_inputs = queries.shape[1]
    request_cache = cached_key_slots.shape[1]
    request_new_tokens = new_token_keys.shape[1]
    query_group_width = QUERY_HEADS // KEY_VALUE_HEADS
    row_count = token_inputs // mlp_count
    request = lookup(placing, slot_index)
    live_len = lookup(cache_len, request)
    query_head_rows = queries[0].reshape(
        token_inputs, KEY_VALUE_HEADS, query_group_width, HEAD_SIZE
    )
    request_keys = cached_key_slots[0].reshape(request_cache, KEY_VALUE_HEADS, HEAD_SIZE)
    request_values = cached_value_slots[0].reshape(request_cache, KEY_VALUE_HEADS, HEAD_SIZE)
    new_key_rows = new_token_keys[0].reshape(request_new_tokens, KEY_VALUE_HEADS, HEAD_SIZE)
    new_value_rows = new_token_values[0].reshape(request_new_tokens, KEY_VALUE_HEADS, HEAD_SIZE)
    cache_pos = mlp_index * request_cache + jnp.arange(request_cache, dtype=jnp.int32)
    cache_live = cache_pos < live_len
    scores_old = (
        jnp.einsum(
            "ngrd,cgd->grnc", query_head_rows, request_keys, preferred_element_type=jnp.float32
        )
        * score_scale
    )
    scores_old = jnp.where(cache_live[None, None, None, :], scores_old, negative)
    fresh_pos = mlp_index * request_new_tokens + jnp.arange(request_new_tokens, dtype=jnp.int32)
    causal = fresh_pos[None, :] <= jnp.arange(token_inputs, dtype=jnp.int32)[:, None]
    scores_new = (
        jnp.einsum(
            "ngrd,mgd->grnm", query_head_rows, new_key_rows, preferred_element_type=jnp.float32
        )
        * score_scale
    )
    scores_new = jnp.where(causal[None, None], scores_new, negative)
    local_top = jnp.maximum(scores_old.max(-1), scores_new.max(-1))
    row_top = lax.pmax(local_top, "mlp")
    expo_old = jnp.exp(scores_old - row_top[..., None])
    expo_new = jnp.exp(scores_new - row_top[..., None])
    denom_local = expo_old.sum(-1) + expo_new.sum(-1)
    probs_old = expo_old.astype(jnp.bfloat16)
    probs_new = expo_new.astype(jnp.bfloat16)
    weighted = jnp.einsum(
        "grnc,cgd->ngrd", probs_old, request_values, preferred_element_type=jnp.float32
    )
    weighted = weighted + jnp.einsum(
        "grnm,mgd->ngrd", probs_new, new_value_rows, preferred_element_type=jnp.float32
    )
    weighted, denom = lax.psum((weighted, denom_local), "mlp")
    attended = (
        (weighted / jnp.transpose(denom, (2, 0, 1))[..., None])
        .reshape(token_inputs, QUERY_HEADS * HEAD_SIZE)
        .astype(jnp.bfloat16)
    )
    normed = rms_rows(attended)
    own_attended = lax.dynamic_slice_in_dim(attended, mlp_index * row_count, row_count, 0)
    gate_sum = jnp.dot(
        normed,
        lax.all_gather(w_gate, "req", axis=0, tiled=True),
        preferred_element_type=jnp.float32,
    )
    upper_sum = jnp.dot(
        normed, lax.all_gather(w_up, "req", axis=0, tiled=True), preferred_element_type=jnp.float32
    )
    hidden = (jax.nn.silu(gate_sum) * upper_sum).astype(jnp.bfloat16)
    partial_down = jnp.dot(
        hidden,
        lax.all_gather(w_down, "req", axis=1, tiled=True),
        preferred_element_type=jnp.float32,
    )
    own_rows = lax.psum_scatter(
        partial_down.astype(jnp.bfloat16), "mlp", scatter_dimension=0, tiled=True
    ).astype(jnp.float32)
    residual = own_attended.astype(jnp.float32)
    return (residual + own_rows).astype(jnp.bfloat16)[None]


CHUNKS = 3
KEY_BLOCK = 512
CACHE_PARTS = 4


def other(index, mask, bits):
    flipped = 0
    for b in range(bits):
        flipped = flipped + ((index // (1 << b) + mask // (1 << b)) % 2) * (1 << b)
    return flipped


def settle(ref, sem):
    pltpu.make_async_copy(ref, ref, sem).wait()


def window_kernel(
    cache_len_ref,
    placing_ref,
    queries_ref,
    keys_ref,
    values_ref,
    new_keys_ref,
    new_values_ref,
    gate_ref,
    upper_ref,
    down_ref,
    out_ref,
    weights,
    keys,
    values,
    queries,
    new_keys,
    new_values,
    weighted,
    top,
    denom,
    share_out,
    share_in,
    own_attended,
    normed,
    total,
    pair_out,
    pair_in,
    chain_out,
    chain_in,
    plane_send,
    plane_recv,
    across_send,
    across_recv,
    core_send,
    core_recv,
    own_sem,
    load_sem,
    cache_sem,
    share_send,
    share_recv,
    token_send,
    token_recv,
    pair_send,
    pair_recv,
    chain_send,
    chain_recv,
):
    slot = lax.axis_index("req")
    core = lax.axis_index("mlp")
    x, p = slot % 2, slot // 2
    y, z = p % 2, p // 2
    beside = p + 1 - 2 * y
    strip = gate_ref.shape[0]
    width = out_ref.shape[1]
    rows = out_ref.shape[0]
    units = gate_ref.shape[1] // 8
    piece = units // CHUNKS
    chunk = 2 * piece
    group = QUERY_HEADS // KEY_VALUE_HEADS
    tokens = 2 * rows

    def at(place, column):
        return {"req": place * 2 + column, "mlp": core}

    def in_plane(place):
        return at(place, x)

    across = at(p, 1 - x)
    twin = {"req": slot, "mlp": 1 - core}

    def push(source, target, send_sem, recv_sem, device):
        pltpu.make_async_remote_copy(
            src_ref=source,
            dst_ref=target,
            send_sem=send_sem,
            recv_sem=recv_sem,
            device_id=device,
            device_id_type=pl.DeviceIdType.MESH,
        ).start()

    barrier = pltpu.get_barrier_semaphore()
    peers = [in_plane(other(p, k, 3)) for k in range(1, 8)] + [across, twin]
    for peer in peers:
        pl.semaphore_signal(barrier, inc=1, device_id=peer, device_id_type=pl.DeviceIdType.MESH)
    pl.semaphore_wait(barrier, len(peers))

    sources = (gate_ref, upper_ref, down_ref)

    def strip_rows(place, column):
        return pl.ds(pl.multiple_of((place * 2 + column) * strip, 16), strip)

    def piece_columns(j, half):
        return pl.ds(pl.multiple_of(j * chunk + half * piece, 128), piece)

    def source_columns(j, place):
        return pl.ds(pl.multiple_of(place * units + j * piece, 128), piece)

    def issue(j, k):
        place = other(p, k, 3)
        for m in range(3):
            push(
                sources[m].at[:, source_columns(j, place)],
                weights.at[m, strip_rows(p, x), piece_columns(j, core)],
                plane_send.at[j],
                plane_recv.at[j, k],
                in_plane(place),
            )

    def issue_own(j):
        for m in range(3):
            source = sources[m].at[:, source_columns(j, p)]
            target = weights.at[m, strip_rows(p, x), piece_columns(j, core)]
            pltpu.make_async_copy(source, target, own_sem).start()
            push(source, target, across_send, across_recv.at[j, 0], across)
            push(source, target, core_send, core_recv.at[j], twin)

    def block_of(j, k, column):
        return weights.at[:, strip_rows(other(p, k, 3), column), piece_columns(j, core)]

    def relay(j, k):
        block = block_of(j, k, x)
        settle(block, plane_recv.at[j, k])
        push(block, block, across_send, across_recv.at[j, k], across)
        push(block, block, core_send, core_recv.at[j], twin)

    def relay_across(j, k):
        block = block_of(j, k, 1 - x)
        settle(block, across_recv.at[j, k])
        push(block, block, core_send, core_recv.at[j], twin)

    def chunk_done(j):
        settle(weights.at[:, :, piece_columns(j, 1 - core)], core_recv.at[j])

    far = [(j, k) for j in range(CHUNKS) for k in (4, 5, 6, 7)]
    near = [(j, k) for j in range(CHUNKS) for k in (1, 2, 3)]

    issue(*far[5])
    issue(*near[1])
    issue(*near[2])
    issue(*far[0])
    issue(*far[10])
    issue(*far[4])
    issue(*near[3])

    part = keys_ref.shape[0] // CACHE_PARTS
    pltpu.make_async_copy(queries_ref, queries, load_sem.at[0]).start()
    pltpu.make_async_copy(new_keys_ref, new_keys, load_sem.at[1]).start()
    pltpu.make_async_copy(new_values_ref, new_values, load_sem.at[2]).start()
    for n in range(CACHE_PARTS):
        span = pl.ds(n * part, part)
        pltpu.make_async_copy(keys_ref.at[span], keys.at[span], cache_sem.at[0, n]).start()
        pltpu.make_async_copy(values_ref.at[span], values.at[span], cache_sem.at[1, n]).start()
    live_len = cache_len_ref[placing_ref[slot]]
    settle(queries, load_sem.at[0])
    settle(new_keys, load_sem.at[1])
    settle(new_values, load_sem.at[2])
    queries[...] = queries[...] * jnp.bfloat16(score_scale)

    def against(a, b):
        return lax.dot_general(
            a, b, (((1,), (1,)), ((), ())), preferred_element_type=jnp.float32
        )

    def lanes(h, size):
        return pl.ds(pl.multiple_of(h * size, 128), size)

    def spread(narrow, size):
        return jnp.concatenate([narrow] * (size // 128), axis=1)

    def folded(wide_rows):
        parts = [wide_rows[:, n : n + 128] for n in range(0, wide_rows.shape[1], 128)]
        while len(parts) > 1:
            parts = [parts[n] + parts[n + 1] for n in range(0, len(parts), 2)]
        return parts[0]

    fresh_pos = core * rows + lax.broadcasted_iota(jnp.int32, (tokens, rows), 1)
    causal = fresh_pos <= lax.broadcasted_iota(jnp.int32, (tokens, rows), 0)
    for h in range(QUERY_HEADS):
        g = h // group
        head = queries[:, h * HEAD_SIZE : (h + 1) * HEAD_SIZE]
        scores = against(head, new_keys[:, g * HEAD_SIZE : (g + 1) * HEAD_SIZE])
        scores = jnp.where(causal, scores, negative)
        row_top = jnp.broadcast_to(jnp.max(scores, axis=1, keepdims=True), (tokens, 128))
        expo = jnp.exp(scores - spread(row_top, rows))
        top[h] = row_top
        denom[h] = folded(expo)
        weighted[h] = jnp.dot(
            expo.astype(jnp.bfloat16),
            new_values[:, g * HEAD_SIZE : (g + 1) * HEAD_SIZE],
            preferred_element_type=jnp.float32,
        )

    def attend_block(g, start):
        span = pl.ds(pl.multiple_of(start, KEY_BLOCK), KEY_BLOCK)
        block_keys = keys[span, lanes(g, HEAD_SIZE)]
        block_values = values[span, lanes(g, HEAD_SIZE)]
        cache_pos = core * keys.shape[0] + start
        live = cache_pos + lax.broadcasted_iota(jnp.int32, (1, KEY_BLOCK), 1) < live_len
        for n in range(group):
            h = g * group + n
            scores = against(queries[:, lanes(h, HEAD_SIZE)], block_keys)
            scores = jnp.where(live, scores, negative)
            old_top = top[h]
            row_top = jnp.maximum(old_top, jnp.max(scores, axis=1, keepdims=True))
            fade = jnp.exp(old_top - row_top)
            expo = jnp.exp(scores - spread(row_top, KEY_BLOCK))
            top[h] = row_top
            denom[h] = denom[h] * fade + folded(expo)
            weighted[h] = weighted[h] * spread(fade, HEAD_SIZE) + jnp.dot(
                expo.astype(jnp.bfloat16), block_values, preferred_element_type=jnp.float32
            )

    def share(h):
        away = pl.ds(pl.multiple_of((1 - core) * rows, rows), rows)
        share_out[h, :, :HEAD_SIZE] = weighted[h, away, :]
        share_out[h, :, HEAD_SIZE : HEAD_SIZE + 128] = top[h, away, :]
        share_out[h, :, HEAD_SIZE + 128 :] = denom[h, away, :]
        push(share_out.at[h], share_in.at[h], share_send, share_recv, twin)

    steps = KEY_VALUE_HEADS * CACHE_PARTS
    def after_0():
        issue(*near[8])
        issue(*near[4])
        for j in range(CHUNKS):
            issue_own(j)

    def after_1():
        issue(*far[1])

    def after_2():
        relay(*near[1])

    def after_3():
        relay(*far[0])
        issue(*near[5])
        relay(*near[3])

    def after_4():
        relay_across(1, 1)

    def after_5():
        issue(*far[3])
        relay(*near[5])
        issue(*near[0])
        issue(*near[6])
        issue(*near[7])
        relay_across(0, 2)
        relay(*far[1])
        issue(*far[8])
        relay(*near[2])

    def after_7():
        relay(*far[10])

    plan = {0: after_0, 1: after_1, 2: after_2, 3: after_3, 4: after_4, 5: after_5, 7: after_7}

    def attend_step(s, carry):
        g, n = s // CACHE_PARTS, s % CACHE_PARTS

        @pl.when(s < CACHE_PARTS)
        def _():
            span = pl.ds(pl.multiple_of(n * part, part), part)
            settle(keys.at[span], cache_sem.at[0, n])
            settle(values.at[span], cache_sem.at[1, n])

        def inner(i, c):
            attend_block(g, n * part + i * KEY_BLOCK)
            return c

        lax.fori_loop(0, part // KEY_BLOCK, inner, 0)

        @pl.when(n == CACHE_PARTS - 1)
        def _():
            for i in range(group):
                share(g * group + i)

        for step, events in plan.items():
            pl.when(s == step)(events)

        return carry

    lax.fori_loop(0, steps, attend_step, 0)

    settle(share_in, share_recv)
    mine = pl.ds(pl.multiple_of(core * rows, rows), rows)
    squares = jnp.zeros((rows, 128), jnp.float32)
    for h in range(QUERY_HEADS):
        own_top, peer_top = top[h, mine, :], share_in[h, :, HEAD_SIZE : HEAD_SIZE + 128]
        row_top = jnp.maximum(own_top, peer_top)
        own_scale, peer_scale = jnp.exp(own_top - row_top), jnp.exp(peer_top - row_top)
        lane_sums = denom[h, mine, :] * own_scale + share_in[h, :, HEAD_SIZE + 128 :] * peer_scale
        head = weighted[h, mine, :] * spread(own_scale, HEAD_SIZE)
        head = head + share_in[h, :, :HEAD_SIZE] * spread(peer_scale, HEAD_SIZE)
        head = (head / jnp.sum(lane_sums, axis=1, keepdims=True)).astype(jnp.bfloat16)
        own_attended[:, h * HEAD_SIZE : (h + 1) * HEAD_SIZE] = head
        wide = head.astype(jnp.float32)
        squares = squares + folded(wide * wide)
    scale = lax.rsqrt(jnp.sum(squares, axis=1, keepdims=True) / width + 1e-06)

    def token_rows(place, count=1):
        return pl.ds(pl.multiple_of(place * rows, rows), count * rows)

    normed[token_rows(p), :] = (own_attended[...].astype(jnp.float32) * scale).astype(jnp.bfloat16)

    def pass_on(place, way, d, device):
        block = normed.at[token_rows(place)]
        push(block, block, token_send.at[way, d], token_recv.at[place], device)

    def sent(place, way, d):
        settle(normed.at[token_rows(place)], token_send.at[way, d])

    def spread_tokens(d):
        below, above = p - 2 * d, p + 2 * d
        if d == 0:
            pl.when(z < 3)(lambda: pass_on(p, 1, 0, in_plane(p + 2)))
            pl.when(z > 0)(lambda: pass_on(p, 2, 0, in_plane(p - 2)))
            pass_on(p, 0, 0, in_plane(beside))
            return

        @pl.when(z >= d)
        def _():
            settle(normed.at[token_rows(below)], token_recv.at[below])
            pl.when(z < 3)(lambda: pass_on(below, 1, d, in_plane(p + 2)))
            pass_on(below, 0, d, in_plane(beside))

        @pl.when(z + d <= 3)
        def _():
            settle(normed.at[token_rows(above)], token_recv.at[above])
            pl.when(z > 0)(lambda: pass_on(above, 2, d, in_plane(p - 2)))
            pass_on(above, 0, 3 + d, in_plane(beside))

    def tokens_sent():
        sent(p, 0, 0)
        pl.when(z < 3)(lambda: sent(p, 1, 0))
        pl.when(z > 0)(lambda: sent(p, 2, 0))
        for d in range(1, 4):
            below, above = p - 2 * d, p + 2 * d
            pl.when(z >= d)(functools.partial(sent, below, 0, d))
            pl.when((z >= d) & (z < 3))(functools.partial(sent, below, 1, d))
            pl.when(z + d <= 3)(functools.partial(sent, above, 0, 3 + d))
            pl.when((z + d <= 3) & (z > 0))(functools.partial(sent, above, 2, d))

    def tokens_here():
        for plane in range(4):
            place = plane * 2 + 1 - y
            settle(normed.at[token_rows(place)], token_recv.at[place])

    def mix(j, span):
        columns = pl.ds(j * chunk, chunk)
        inputs = normed[span, :]
        gate_sum = jnp.dot(inputs, weights[0, :, columns], preferred_element_type=jnp.float32)
        upper_sum = jnp.dot(inputs, weights[1, :, columns], preferred_element_type=jnp.float32)
        hidden = (gate_sum / (1.0 + jnp.exp(-gate_sum)) * upper_sum).astype(jnp.bfloat16)
        return against(hidden, weights[2, :, columns])

    half_rows = 4 * rows

    def early(j, half):
        span = pl.ds(half * half_rows, half_rows)
        if j == 0:
            total[span, :] = mix(j, span)
        else:
            total[span, :] += mix(j, span)

    spread_tokens(0)
    relay(*far[8])
    relay(*near[7])
    relay(*near[6])
    relay_across(2, 2)
    spread_tokens(1)
    relay_across(0, 3)
    relay(*far[4])
    relay(*near[0])
    relay_across(0, 1)
    relay(*far[3])
    relay(*near[4])
    relay(*far[5])
    issue(*far[2])
    spread_tokens(2)
    relay(*far[2])
    relay_across(*far[0])
    relay_across(*far[3])
    issue(*far[7])
    relay_across(*far[1])
    relay_across(0, 0)
    spread_tokens(3)
    relay_across(1, 2)
    issue(*far[6])
    relay_across(*far[10])
    relay(*near[8])
    relay_across(2, 3)
    issue(*far[11])
    relay_across(1, 3)
    relay(*far[7])
    relay_across(*far[7])
    relay_across(1, 0)
    relay_across(2, 1)
    relay_across(*far[5])
    relay_across(2, 0)
    relay_across(*far[2])
    relay(*far[6])
    relay_across(*far[4])
    settle(weights.at[:, pl.ds(0, strip), pl.ds(0, units)], own_sem)
    chunk_done(0)
    relay_across(*far[8])
    issue(*far[9])
    tokens_here()
    early(0, 0)
    relay_across(*far[6])
    chunk_done(1)
    relay(*far[11])
    early(0, 1)
    relay(*far[9])
    early(1, 0)
    early(1, 1)
    relay_across(*far[9])
    relay_across(*far[11])
    chunk_done(2)

    upper_half = z // 2
    folded_z = z + upper_half * (3 - 2 * z)

    def plane_of(i):
        base = (3, 2, 1 - folded_z, folded_z)[i]
        return base + upper_half * (3 - 2 * base)

    def last(i):
        plane = plane_of(i)
        span = token_rows(plane * 2, 2)
        total[span, :] += mix(CHUNKS - 1, span)
        pair_out[i] = total[token_rows(plane * 2 + 1 - y), :].astype(jnp.bfloat16)
        push(pair_out.at[i], pair_in.at[i], pair_send.at[i], pair_recv.at[i], in_plane(beside))

    def column_sum(i):
        settle(pair_in.at[i], pair_recv.at[i])
        own = token_rows(plane_of(i) * 2 + y)
        total[own, :] += pair_in[i].astype(jnp.float32)
        return own

    def add_chain(own, way, plane):
        settle(chain_in.at[way, plane], chain_recv.at[way, plane])
        total[own, :] += chain_in[way, plane].astype(jnp.float32)

    def along(i):
        plane = plane_of(i)
        own = column_sum(i)

        def go(way, device, has_more):
            @pl.when(has_more)
            def _():
                add_chain(own, way, plane)

            chain_out[i] = total[own, :].astype(jnp.bfloat16)
            push(
                chain_out.at[i],
                chain_in.at[way, plane],
                chain_send.at[i],
                chain_recv.at[way, plane],
                device,
            )

        pl.when(plane > z)(lambda: go(0, in_plane(p + 2), z > 0))
        pl.when(plane < z)(lambda: go(1, in_plane(p - 2), z < 3))

    last(0)
    last(1)
    last(2)
    along(0)
    last(3)
    along(1)
    along(2)
    own = column_sum(3)
    pl.when(z > 0)(lambda: add_chain(own, 0, z))
    pl.when(z < 3)(lambda: add_chain(own, 1, z))
    out_ref[...] = (own_attended[...].astype(jnp.float32) + total[own, :]).astype(jnp.bfloat16)

    for j in range(CHUNKS):
        settle(weights.at[:, pl.ds(0, 7 * strip), pl.ds(0, piece)], plane_send.at[j])
    settle(weights.at[:, pl.ds(0, 8 * strip), pl.ds(0, units)], across_send)
    settle(weights.at[:, :, pl.ds(0, units)], core_send)
    settle(share_out, share_send)
    tokens_sent()
    for i in range(4):
        settle(pair_out.at[i], pair_send.at[i])
    for i in range(3):
        settle(chain_out.at[i], chain_send.at[i])


def window(
    queries,
    cached_key_slots,
    cached_value_slots,
    new_token_keys,
    new_token_values,
    cache_len,
    placing,
    w_gate,
    w_up,
    w_down,
):
    tokens, width = queries.shape
    rows = tokens // 2
    bf16, f32 = jnp.bfloat16, jnp.float32
    vmem, dma = pltpu.VMEM, pltpu.SemaphoreType.DMA
    hidden_units = w_gate.shape[1] // 4
    scalars = pl.BlockSpec(memory_space=pltpu.SMEM)
    return pl.pallas_call(
        window_kernel,
        out_shape=jax.ShapeDtypeStruct((rows, width), bf16),
        in_specs=[scalars] * 2 + [pl.BlockSpec(memory_space=pl.ANY)] * 8,
        out_specs=pl.BlockSpec(memory_space=pltpu.VMEM),
        scratch_shapes=[
            vmem((3, width, hidden_units), bf16),
            vmem(cached_key_slots.shape, bf16),
            vmem(cached_value_slots.shape, bf16),
            vmem((tokens, width), bf16),
            vmem(new_token_keys.shape, bf16),
            vmem(new_token_values.shape, bf16),
            vmem((QUERY_HEADS, tokens, HEAD_SIZE), f32),
            vmem((QUERY_HEADS, tokens, 128), f32),
            vmem((QUERY_HEADS, tokens, 128), f32),
            vmem((QUERY_HEADS, rows, 2 * HEAD_SIZE), f32),
            vmem((QUERY_HEADS, rows, 2 * HEAD_SIZE), f32),
            vmem((rows, width), bf16),
            vmem((8 * rows, width), bf16),
            vmem((8 * rows, width), f32),
            vmem((4, rows, width), bf16),
            vmem((4, rows, width), bf16),
            vmem((3, rows, width), bf16),
            vmem((2, 4, rows, width), bf16),
            dma((CHUNKS,)),
            dma((CHUNKS, 8)),
            dma,
            dma((CHUNKS, 8)),
            dma,
            dma((CHUNKS,)),
            dma,
            dma((3,)),
            dma((2, CACHE_PARTS)),
            dma,
            dma,
            dma((3, 7)),
            dma((8,)),
            dma((4,)),
            dma((4,)),
            dma((3,)),
            dma((2, 4)),
        ],
        compiler_params=pltpu.CompilerParams(
            collective_id=0, has_side_effects=True, vmem_limit_bytes=60 * 1024 * 1024
        ),
        name="window",
    )(
        cache_len,
        placing,
        queries,
        cached_key_slots,
        cached_value_slots,
        new_token_keys,
        new_token_values,
        w_gate,
        w_up,
        w_down.T,
    )


def body(
    queries,
    cached_key_slots,
    cached_value_slots,
    new_token_keys,
    new_token_values,
    cache_len,
    placing,
    w_gate,
    w_up,
    w_down,
):
    if lax.axis_size("req") != 16 or lax.axis_size("mlp") != 2:
        return wide_body(
            queries,
            cached_key_slots,
            cached_value_slots,
            new_token_keys,
            new_token_values,
            cache_len,
            placing,
            w_gate,
            w_up,
            w_down,
        )
    return window(
        queries[0],
        cached_key_slots[0],
        cached_value_slots[0],
        new_token_keys[0],
        new_token_values[0],
        cache_len,
        placing,
        w_gate,
        w_up,
        w_down,
    )[None]


def solution(mesh):
    in_specs = (
        P("req", None, None),
        P("req", "mlp", None),
        P("req", "mlp", None),
        P("req", "mlp", None),
        P("req", "mlp", None),
        P(),
        P(),
        P("req", "mlp"),
        P("req", "mlp"),
        P("mlp", "req"),
    )
    out_specs = P("req", "mlp", None)
    return jax.shard_map(body, mesh=mesh, in_specs=in_specs, out_specs=out_specs, check_vma=False)
```

```python
import functools

import jax
import jax.numpy as jnp
from jax import lax
from jax.experimental import pallas as pl
from jax.experimental.pallas import tpu as pltpu
from jax.sharding import PartitionSpec as P

HEAD_SIZE = 256
QUERY_HEADS = 6
KEY_VALUE_HEADS = 2


score_scale = 0.0625
negative = -1e30


def lookup(table, index):
    positions = jnp.arange(table.shape[0], dtype=jnp.int32)
    return jnp.sum(jnp.where(positions == index, table, 0))


def rms_rows(attended):
    wide = attended.astype(jnp.float32)
    return (wide * lax.rsqrt(jnp.mean(wide * wide, axis=-1, keepdims=True) + 1e-06)).astype(
        jnp.bfloat16
    )


def wide_body(
    queries,
    cached_key_slots,
    cached_value_slots,
    new_token_keys,
    new_token_values,
    cache_len,
    placing,
    w_gate,
    w_up,
    w_down,
):
    slot_index = lax.axis_index("req")
    mlp_index = lax.axis_index("mlp")
    mlp_count = lax.axis_size("mlp")
    token_inputs = queries.shape[1]
    request_cache = cached_key_slots.shape[1]
    request_new_tokens = new_token_keys.shape[1]
    query_group_width = QUERY_HEADS // KEY_VALUE_HEADS
    row_count = token_inputs // mlp_count
    request = lookup(placing, slot_index)
    live_len = lookup(cache_len, request)
    query_head_rows = queries[0].reshape(
        token_inputs, KEY_VALUE_HEADS, query_group_width, HEAD_SIZE
    )
    request_keys = cached_key_slots[0].reshape(request_cache, KEY_VALUE_HEADS, HEAD_SIZE)
    request_values = cached_value_slots[0].reshape(request_cache, KEY_VALUE_HEADS, HEAD_SIZE)
    new_key_rows = new_token_keys[0].reshape(request_new_tokens, KEY_VALUE_HEADS, HEAD_SIZE)
    new_value_rows = new_token_values[0].reshape(request_new_tokens, KEY_VALUE_HEADS, HEAD_SIZE)
    cache_pos = mlp_index * request_cache + jnp.arange(request_cache, dtype=jnp.int32)
    cache_live = cache_pos < live_len
    scores_old = (
        jnp.einsum(
            "ngrd,cgd->grnc", query_head_rows, request_keys, preferred_element_type=jnp.float32
        )
        * score_scale
    )
    scores_old = jnp.where(cache_live[None, None, None, :], scores_old, negative)
    fresh_pos = mlp_index * request_new_tokens + jnp.arange(request_new_tokens, dtype=jnp.int32)
    causal = fresh_pos[None, :] <= jnp.arange(token_inputs, dtype=jnp.int32)[:, None]
    scores_new = (
        jnp.einsum(
            "ngrd,mgd->grnm", query_head_rows, new_key_rows, preferred_element_type=jnp.float32
        )
        * score_scale
    )
    scores_new = jnp.where(causal[None, None], scores_new, negative)
    local_top = jnp.maximum(scores_old.max(-1), scores_new.max(-1))
    row_top = lax.pmax(local_top, "mlp")
    expo_old = jnp.exp(scores_old - row_top[..., None])
    expo_new = jnp.exp(scores_new - row_top[..., None])
    denom_local = expo_old.sum(-1) + expo_new.sum(-1)
    probs_old = expo_old.astype(jnp.bfloat16)
    probs_new = expo_new.astype(jnp.bfloat16)
    weighted = jnp.einsum(
        "grnc,cgd->ngrd", probs_old, request_values, preferred_element_type=jnp.float32
    )
    weighted = weighted + jnp.einsum(
        "grnm,mgd->ngrd", probs_new, new_value_rows, preferred_element_type=jnp.float32
    )
    weighted, denom = lax.psum((weighted, denom_local), "mlp")
    attended = (
        (weighted / jnp.transpose(denom, (2, 0, 1))[..., None])
        .reshape(token_inputs, QUERY_HEADS * HEAD_SIZE)
        .astype(jnp.bfloat16)
    )
    normed = rms_rows(attended)
    own_attended = lax.dynamic_slice_in_dim(attended, mlp_index * row_count, row_count, 0)
    gate_sum = jnp.dot(
        normed,
        lax.all_gather(w_gate, "req", axis=0, tiled=True),
        preferred_element_type=jnp.float32,
    )
    upper_sum = jnp.dot(
        normed, lax.all_gather(w_up, "req", axis=0, tiled=True), preferred_element_type=jnp.float32
    )
    hidden = (jax.nn.silu(gate_sum) * upper_sum).astype(jnp.bfloat16)
    partial_down = jnp.dot(
        hidden,
        lax.all_gather(w_down, "req", axis=1, tiled=True),
        preferred_element_type=jnp.float32,
    )
    own_rows = lax.psum_scatter(
        partial_down.astype(jnp.bfloat16), "mlp", scatter_dimension=0, tiled=True
    ).astype(jnp.float32)
    residual = own_attended.astype(jnp.float32)
    return (residual + own_rows).astype(jnp.bfloat16)[None]


CHUNKS = 3
KEY_BLOCK = 512
CACHE_PARTS = 4


def other(index, mask, bits):
    flipped = 0
    for b in range(bits):
        flipped = flipped + ((index // (1 << b) + mask // (1 << b)) % 2) * (1 << b)
    return flipped


def settle(ref, sem):
    pltpu.make_async_copy(ref, ref, sem).wait()


def window_kernel(
    cache_len_ref,
    placing_ref,
    queries_ref,
    keys_ref,
    values_ref,
    new_keys_ref,
    new_values_ref,
    gate_ref,
    upper_ref,
    down_ref,
    out_ref,
    weights,
    keys,
    values,
    queries,
    new_keys,
    new_values,
    weighted,
    top,
    denom,
    share_out,
    share_in,
    own_attended,
    normed,
    total,
    pair_out,
    pair_in,
    chain_out,
    chain_in,
    late_out,
    late_in,
    late_pair_out,
    late_pair_in,
    plane_send,
    plane_recv,
    across_send,
    across_recv,
    core_send,
    core_recv,
    own_sem,
    load_sem,
    cache_sem,
    share_send,
    share_recv,
    token_send,
    token_recv,
    pair_send,
    pair_recv,
    chain_send,
    chain_recv,
    late_send,
    late_recv,
    late_pair_send,
    late_pair_recv,
):
    slot = lax.axis_index("req")
    core = lax.axis_index("mlp")
    x, p = slot % 2, slot // 2
    y, z = p % 2, p // 2
    beside = p + 1 - 2 * y
    strip = gate_ref.shape[0]
    width = out_ref.shape[1]
    rows = out_ref.shape[0]
    units = gate_ref.shape[1] // 8
    piece = units // CHUNKS
    chunk = 2 * piece
    group = QUERY_HEADS // KEY_VALUE_HEADS
    tokens = 2 * rows

    def at(place, column):
        return {"req": place * 2 + column, "mlp": core}

    def in_plane(place):
        return at(place, x)

    across = at(p, 1 - x)
    twin = {"req": slot, "mlp": 1 - core}

    def push(source, target, send_sem, recv_sem, device):
        pltpu.make_async_remote_copy(
            src_ref=source,
            dst_ref=target,
            send_sem=send_sem,
            recv_sem=recv_sem,
            device_id=device,
            device_id_type=pl.DeviceIdType.MESH,
        ).start()

    barrier = pltpu.get_barrier_semaphore()
    peers = [in_plane(other(p, k, 3)) for k in range(1, 8)] + [across, twin]
    for peer in peers:
        pl.semaphore_signal(barrier, inc=1, device_id=peer, device_id_type=pl.DeviceIdType.MESH)
    pl.semaphore_wait(barrier, len(peers))

    sources = (gate_ref, upper_ref, down_ref)

    def strip_rows(place, column):
        return pl.ds(pl.multiple_of((place * 2 + column) * strip, 16), strip)

    def piece_columns(j, half):
        return pl.ds(pl.multiple_of(j * chunk + half * piece, 128), piece)

    def source_columns(j, place):
        return pl.ds(pl.multiple_of(place * units + j * piece, 128), piece)

    def issue(j, k):
        place = other(p, k, 3)
        for m in range(3):
            push(
                sources[m].at[:, source_columns(j, place)],
                weights.at[m, strip_rows(p, x), piece_columns(j, core)],
                plane_send.at[j],
                plane_recv.at[j, k],
                in_plane(place),
            )

    def issue_own(j):
        for m in range(3):
            source = sources[m].at[:, source_columns(j, p)]
            target = weights.at[m, strip_rows(p, x), piece_columns(j, core)]
            pltpu.make_async_copy(source, target, own_sem).start()
            push(source, target, across_send, across_recv.at[j, 0], across)
            push(source, target, core_send, core_recv.at[j], twin)

    def block_of(j, k, column):
        return weights.at[:, strip_rows(other(p, k, 3), column), piece_columns(j, core)]

    def relay(j, k):
        block = block_of(j, k, x)
        settle(block, plane_recv.at[j, k])
        push(block, block, across_send, across_recv.at[j, k], across)
        push(block, block, core_send, core_recv.at[j], twin)

    def relay_across(j, k):
        block = block_of(j, k, 1 - x)
        settle(block, across_recv.at[j, k])
        push(block, block, core_send, core_recv.at[j], twin)

    def chunk_done(j):
        settle(weights.at[:, :, piece_columns(j, 1 - core)], core_recv.at[j])

    far = [(j, k) for j in range(CHUNKS) for k in (4, 5, 6, 7)]
    near = [(j, k) for j in range(CHUNKS) for k in (1, 2, 3)]

    issue(*near[2])
    issue(*far[0])

    part = keys_ref.shape[0] // CACHE_PARTS
    pltpu.make_async_copy(queries_ref, queries, load_sem.at[0]).start()
    pltpu.make_async_copy(new_keys_ref, new_keys, load_sem.at[1]).start()
    pltpu.make_async_copy(new_values_ref, new_values, load_sem.at[2]).start()
    for n in range(CACHE_PARTS):
        span = pl.ds(n * part, part)
        pltpu.make_async_copy(keys_ref.at[span], keys.at[span], cache_sem.at[0, n]).start()
        pltpu.make_async_copy(values_ref.at[span], values.at[span], cache_sem.at[1, n]).start()
    live_len = cache_len_ref[placing_ref[slot]]
    settle(queries, load_sem.at[0])
    settle(new_keys, load_sem.at[1])
    settle(new_values, load_sem.at[2])
    queries[...] = queries[...] * jnp.bfloat16(score_scale)

    def against(a, b):
        return lax.dot_general(
            a, b, (((1,), (1,)), ((), ())), preferred_element_type=jnp.float32
        )

    def lanes(h, size):
        return pl.ds(pl.multiple_of(h * size, 128), size)

    def spread(narrow, size):
        return jnp.concatenate([narrow] * (size // 128), axis=1)

    def folded(wide_rows):
        parts = [wide_rows[:, n : n + 128] for n in range(0, wide_rows.shape[1], 128)]
        while len(parts) > 1:
            parts = [parts[n] + parts[n + 1] for n in range(0, len(parts), 2)]
        return parts[0]

    fresh_pos = core * rows + lax.broadcasted_iota(jnp.int32, (tokens, rows), 1)
    causal = fresh_pos <= lax.broadcasted_iota(jnp.int32, (tokens, rows), 0)
    for h in range(QUERY_HEADS):
        g = h // group
        head = queries[:, h * HEAD_SIZE : (h + 1) * HEAD_SIZE]
        scores = against(head, new_keys[:, g * HEAD_SIZE : (g + 1) * HEAD_SIZE])
        scores = jnp.where(causal, scores, negative)
        row_top = jnp.broadcast_to(jnp.max(scores, axis=1, keepdims=True), (tokens, 128))
        expo = jnp.exp(scores - spread(row_top, rows))
        top[h] = row_top
        denom[h] = folded(expo)
        weighted[h] = jnp.dot(
            expo.astype(jnp.bfloat16),
            new_values[:, g * HEAD_SIZE : (g + 1) * HEAD_SIZE],
            preferred_element_type=jnp.float32,
        )

    def attend_block(g, start):
        span = pl.ds(pl.multiple_of(start, KEY_BLOCK), KEY_BLOCK)
        block_keys = keys[span, lanes(g, HEAD_SIZE)]
        block_values = values[span, lanes(g, HEAD_SIZE)]
        cache_pos = core * keys.shape[0] + start
        live = cache_pos + lax.broadcasted_iota(jnp.int32, (1, KEY_BLOCK), 1) < live_len
        for n in range(group):
            h = g * group + n
            scores = against(queries[:, lanes(h, HEAD_SIZE)], block_keys)
            scores = jnp.where(live, scores, negative)
            old_top = top[h]
            row_top = jnp.maximum(old_top, jnp.max(scores, axis=1, keepdims=True))
            fade = jnp.exp(old_top - row_top)
            expo = jnp.exp(scores - spread(row_top, KEY_BLOCK))
            top[h] = row_top
            denom[h] = denom[h] * fade + folded(expo)
            weighted[h] = weighted[h] * spread(fade, HEAD_SIZE) + jnp.dot(
                expo.astype(jnp.bfloat16), block_values, preferred_element_type=jnp.float32
            )

    def share(h):
        away = pl.ds(pl.multiple_of((1 - core) * rows, rows), rows)
        share_out[h, :, :HEAD_SIZE] = weighted[h, away, :]
        share_out[h, :, HEAD_SIZE : HEAD_SIZE + 128] = top[h, away, :]
        share_out[h, :, HEAD_SIZE + 128 :] = denom[h, away, :]
        push(share_out.at[h], share_in.at[h], share_send, share_recv, twin)

    steps = KEY_VALUE_HEADS * CACHE_PARTS
    def after_1():
        issue(*far[1])
        issue(*near[6])
        issue(*near[0])
        issue(*near[7])
        issue(*far[5])
        relay(*near[2])
        relay_across(0, 3)
        issue(*near[4])
        issue(*far[4])
        for j in range(CHUNKS):
            issue_own(j)
        issue(*near[1])

    def after_2():
        issue(*near[8])
        relay(*near[7])

    def after_4():
        issue(*far[3])

    def after_5():
        relay(*near[4])

    def after_6():
        issue(*far[10])
        relay(*far[1])
        issue(*near[5])
        relay(*near[1])
        relay_across(1, 0)
        relay(*far[4])
        relay(*near[8])

    def after_7():
        relay(*far[3])

    plan = {1: after_1, 2: after_2, 4: after_4, 5: after_5, 6: after_6, 7: after_7}

    def attend_step(s, carry):
        g, n = s // CACHE_PARTS, s % CACHE_PARTS

        @pl.when(s < CACHE_PARTS)
        def _():
            span = pl.ds(pl.multiple_of(n * part, part), part)
            settle(keys.at[span], cache_sem.at[0, n])
            settle(values.at[span], cache_sem.at[1, n])

        def inner(i, c):
            attend_block(g, n * part + i * KEY_BLOCK)
            return c

        lax.fori_loop(0, part // KEY_BLOCK, inner, 0)

        @pl.when(n == CACHE_PARTS - 1)
        def _():
            for i in range(group):
                share(g * group + i)

        for step, events in plan.items():
            pl.when(s == step)(events)

        return carry

    lax.fori_loop(0, steps, attend_step, 0)

    settle(share_in, share_recv)
    mine = pl.ds(pl.multiple_of(core * rows, rows), rows)
    squares = jnp.zeros((rows, 128), jnp.float32)
    for h in range(QUERY_HEADS):
        own_top, peer_top = top[h, mine, :], share_in[h, :, HEAD_SIZE : HEAD_SIZE + 128]
        row_top = jnp.maximum(own_top, peer_top)
        own_scale, peer_scale = jnp.exp(own_top - row_top), jnp.exp(peer_top - row_top)
        lane_sums = denom[h, mine, :] * own_scale + share_in[h, :, HEAD_SIZE + 128 :] * peer_scale
        head = weighted[h, mine, :] * spread(own_scale, HEAD_SIZE)
        head = head + share_in[h, :, :HEAD_SIZE] * spread(peer_scale, HEAD_SIZE)
        head = (head / jnp.sum(lane_sums, axis=1, keepdims=True)).astype(jnp.bfloat16)
        own_attended[:, h * HEAD_SIZE : (h + 1) * HEAD_SIZE] = head
        wide = head.astype(jnp.float32)
        squares = squares + folded(wide * wide)
    scale = lax.rsqrt(jnp.sum(squares, axis=1, keepdims=True) / width + 1e-06)

    def token_rows(place, count=1):
        return pl.ds(pl.multiple_of(place * rows, rows), count * rows)

    normed[token_rows(p), :] = (own_attended[...].astype(jnp.float32) * scale).astype(jnp.bfloat16)

    def pass_on(place, way, d, device):
        block = normed.at[token_rows(place)]
        push(block, block, token_send.at[way, d], token_recv.at[place], device)

    def sent(place, way, d):
        settle(normed.at[token_rows(place)], token_send.at[way, d])

    def spread_tokens(d):
        below, above = p - 2 * d, p + 2 * d
        if d == 0:
            pl.when(z < 3)(lambda: pass_on(p, 1, 0, in_plane(p + 2)))
            pl.when(z > 0)(lambda: pass_on(p, 2, 0, in_plane(p - 2)))
            pass_on(p, 0, 0, in_plane(beside))
            return

        @pl.when(z >= d)
        def _():
            settle(normed.at[token_rows(below)], token_recv.at[below])
            pl.when(z < 3)(lambda: pass_on(below, 1, d, in_plane(p + 2)))
            pass_on(below, 0, d, in_plane(beside))

        @pl.when(z + d <= 3)
        def _():
            settle(normed.at[token_rows(above)], token_recv.at[above])
            pl.when(z > 0)(lambda: pass_on(above, 2, d, in_plane(p - 2)))
            pass_on(above, 0, 3 + d, in_plane(beside))

    def tokens_sent():
        sent(p, 0, 0)
        pl.when(z < 3)(lambda: sent(p, 1, 0))
        pl.when(z > 0)(lambda: sent(p, 2, 0))
        for d in range(1, 4):
            below, above = p - 2 * d, p + 2 * d
            pl.when(z >= d)(functools.partial(sent, below, 0, d))
            pl.when((z >= d) & (z < 3))(functools.partial(sent, below, 1, d))
            pl.when(z + d <= 3)(functools.partial(sent, above, 0, 3 + d))
            pl.when((z + d <= 3) & (z > 0))(functools.partial(sent, above, 2, d))

    def tokens_here():
        for plane in range(4):
            place = plane * 2 + 1 - y
            settle(normed.at[token_rows(place)], token_recv.at[place])

    def mix(j, span):
        columns = pl.ds(j * chunk, chunk)
        inputs = normed[span, :]
        gate_sum = jnp.dot(inputs, weights[0, :, columns], preferred_element_type=jnp.float32)
        upper_sum = jnp.dot(inputs, weights[1, :, columns], preferred_element_type=jnp.float32)
        hidden = (gate_sum / (1.0 + jnp.exp(-gate_sum)) * upper_sum).astype(jnp.bfloat16)
        return against(hidden, weights[2, :, columns])

    half_rows = 4 * rows

    def early(j, half):
        span = pl.ds(half * half_rows, half_rows)
        if j == 0:
            total[span, :] = mix(j, span)
        else:
            total[span, :] += mix(j, span)

    spread_tokens(0)
    issue(*far[7])
    relay_across(0, 0)
    issue(*near[3])
    relay(*near[6])
    relay(*far[7])
    relay(*far[5])
    spread_tokens(1)
    relay_across(0, 2)
    relay_across(2, 0)
    relay_across(1, 2)
    relay(*far[0])
    relay(*near[3])
    relay_across(*far[3])
    relay(*near[0])
    relay_across(2, 3)
    relay(*near[5])
    spread_tokens(2)
    issue(*far[2])
    relay_across(1, 1)
    relay_across(2, 1)
    issue(*far[9])
    issue(*far[8])
    relay(*far[2])
    relay(*far[10])
    spread_tokens(3)
    relay_across(*far[2])
    relay_across(*far[7])
    relay_across(0, 1)
    relay_across(1, 3)
    relay_across(*far[4])
    relay_across(*far[0])
    relay(*far[8])
    issue(*far[6])
    relay_across(2, 2)
    relay_across(*far[1])
    relay(*far[9])
    settle(weights.at[:, pl.ds(0, strip), pl.ds(0, units)], own_sem)
    chunk_done(0)
    relay_across(*far[10])
    relay_across(*far[5])
    relay_across(*far[8])
    tokens_here()
    issue(*far[11])
    relay(*far[6])
    early(0, 0)
    early(0, 1)
    relay_across(*far[9])
    relay_across(*far[6])
    chunk_done(1)
    relay(*far[11])
    early(1, 0)
    early(1, 1)
    relay_across(*far[11])
    chunk_done(2)

    upper_half = z // 2
    folded_z = z + upper_half * (3 - 2 * z)

    def plane_of(i):
        base = (3, 2, 1 - folded_z, folded_z)[i]
        return base + upper_half * (3 - 2 * base)

    front = pair_out.shape[2]
    early_lanes, late_lanes = pl.ds(0, front), pl.ds(front, width - front)

    def last(i):
        plane = plane_of(i)
        span = token_rows(plane * 2, 2)
        total[span, :] += mix(CHUNKS - 1, span)
        away = token_rows(plane * 2 + 1 - y)
        pair_out[i] = total[away, early_lanes].astype(jnp.bfloat16)
        push(pair_out.at[i], pair_in.at[i], pair_send.at[i], pair_recv.at[i], in_plane(beside))

    def column_sum(i):
        settle(pair_in.at[i], pair_recv.at[i])
        own = token_rows(plane_of(i) * 2 + y)
        total[own, early_lanes] += pair_in[i].astype(jnp.float32)
        return own

    def add_early(span, way, plane):
        settle(chain_in.at[way, plane], chain_recv.at[way, plane])
        total[span, early_lanes] += chain_in[way, plane].astype(jnp.float32)

    def add_late(span, way, plane):
        settle(late_in.at[way, plane], late_recv.at[way, plane])
        total[span, late_lanes] += late_in[way, plane].astype(jnp.float32)

    def onward(i, span, lanes_of, add, out, into, send_sem, recv_sem):
        plane = plane_of(i)

        def go(way, device, has_more):
            @pl.when(has_more)
            def _():
                add(span, way, plane)

            out[i] = total[span, lanes_of].astype(jnp.bfloat16)
            push(out.at[i], into.at[way, plane], send_sem.at[i], recv_sem.at[way, plane], device)

        pl.when(plane > z)(lambda: go(0, in_plane(p + 2), z > 0))
        pl.when(plane < z)(lambda: go(1, in_plane(p - 2), z < 3))

    def along(i):
        own = column_sum(i)
        onward(i, own, early_lanes, add_early, chain_out, chain_in, chain_send, chain_recv)

    def along_late(i):
        span = token_rows(plane_of(i) * 2, 2)
        onward(i, span, late_lanes, add_late, late_out, late_in, late_send, late_recv)

    def settle_late():
        span = token_rows(z * 2, 2)
        pl.when(z > 0)(lambda: add_late(span, 0, z))
        pl.when(z < 3)(lambda: add_late(span, 1, z))
        late_pair_out[...] = total[token_rows(beside), late_lanes].astype(jnp.bfloat16)
        push(late_pair_out, late_pair_in, late_pair_send, late_pair_recv, in_plane(beside))

    last(0)
    last(1)
    along_late(0)
    last(2)
    along_late(1)
    last(3)
    along_late(2)
    along(0)
    along(1)
    settle_late()
    along(2)
    own = column_sum(3)
    pl.when(z > 0)(lambda: add_early(own, 0, z))
    pl.when(z < 3)(lambda: add_early(own, 1, z))
    settle(late_pair_in, late_pair_recv)
    total[own, late_lanes] += late_pair_in[...].astype(jnp.float32)
    out_ref[...] = (own_attended[...].astype(jnp.float32) + total[own, :]).astype(jnp.bfloat16)

    for j in range(CHUNKS):
        settle(weights.at[:, pl.ds(0, 7 * strip), pl.ds(0, piece)], plane_send.at[j])
    settle(weights.at[:, pl.ds(0, 8 * strip), pl.ds(0, units)], across_send)
    settle(weights.at[:, :, pl.ds(0, units)], core_send)
    settle(share_out, share_send)
    tokens_sent()
    for i in range(4):
        settle(pair_out.at[i], pair_send.at[i])
    for i in range(3):
        settle(chain_out.at[i], chain_send.at[i])
        settle(late_out.at[i], late_send.at[i])
    settle(late_pair_out, late_pair_send)


def window(
    queries,
    cached_key_slots,
    cached_value_slots,
    new_token_keys,
    new_token_values,
    cache_len,
    placing,
    w_gate,
    w_up,
    w_down,
):
    tokens, width = queries.shape
    rows = tokens // 2
    bf16, f32 = jnp.bfloat16, jnp.float32
    vmem, dma = pltpu.VMEM, pltpu.SemaphoreType.DMA
    hidden_units = w_gate.shape[1] // 4
    late = width // 6
    scalars = pl.BlockSpec(memory_space=pltpu.SMEM)
    return pl.pallas_call(
        window_kernel,
        out_shape=jax.ShapeDtypeStruct((rows, width), bf16),
        in_specs=[scalars] * 2 + [pl.BlockSpec(memory_space=pl.ANY)] * 8,
        out_specs=pl.BlockSpec(memory_space=pltpu.VMEM),
        scratch_shapes=[
            vmem((3, width, hidden_units), bf16),
            vmem(cached_key_slots.shape, bf16),
            vmem(cached_value_slots.shape, bf16),
            vmem((tokens, width), bf16),
            vmem(new_token_keys.shape, bf16),
            vmem(new_token_values.shape, bf16),
            vmem((QUERY_HEADS, tokens, HEAD_SIZE), f32),
            vmem((QUERY_HEADS, tokens, 128), f32),
            vmem((QUERY_HEADS, tokens, 128), f32),
            vmem((QUERY_HEADS, rows, 2 * HEAD_SIZE), f32),
            vmem((QUERY_HEADS, rows, 2 * HEAD_SIZE), f32),
            vmem((rows, width), bf16),
            vmem((8 * rows, width), bf16),
            vmem((8 * rows, width), f32),
            vmem((4, rows, width - late), bf16),
            vmem((4, rows, width - late), bf16),
            vmem((3, rows, width - late), bf16),
            vmem((2, 4, rows, width - late), bf16),
            vmem((3, tokens, late), bf16),
            vmem((2, 4, tokens, late), bf16),
            vmem((rows, late), bf16),
            vmem((rows, late), bf16),
            dma((CHUNKS,)),
            dma((CHUNKS, 8)),
            dma,
            dma((CHUNKS, 8)),
            dma,
            dma((CHUNKS,)),
            dma,
            dma((3,)),
            dma((2, CACHE_PARTS)),
            dma,
            dma,
            dma((3, 7)),
            dma((8,)),
            dma((4,)),
            dma((4,)),
            dma((3,)),
            dma((2, 4)),
            dma((3,)),
            dma((2, 4)),
            dma,
            dma,
        ],
        compiler_params=pltpu.CompilerParams(
            collective_id=0, has_side_effects=True, vmem_limit_bytes=60 * 1024 * 1024
        ),
        name="window",
    )(
        cache_len,
        placing,
        queries,
        cached_key_slots,
        cached_value_slots,
        new_token_keys,
        new_token_values,
        w_gate,
        w_up,
        w_down.T,
    )


def body(
    queries,
    cached_key_slots,
    cached_value_slots,
    new_token_keys,
    new_token_values,
    cache_len,
    placing,
    w_gate,
    w_up,
    w_down,
):
    if lax.axis_size("req") != 16 or lax.axis_size("mlp") != 2:
        return wide_body(
            queries,
            cached_key_slots,
            cached_value_slots,
            new_token_keys,
            new_token_values,
            cache_len,
            placing,
            w_gate,
            w_up,
            w_down,
        )
    return window(
        queries[0],
        cached_key_slots[0],
        cached_value_slots[0],
        new_token_keys[0],
        new_token_values[0],
        cache_len,
        placing,
        w_gate,
        w_up,
        w_down,
    )[None]


def solution(mesh):
    in_specs = (
        P("req", None, None),
        P("req", "mlp", None),
        P("req", "mlp", None),
        P("req", "mlp", None),
        P("req", "mlp", None),
        P(),
        P(),
        P("req", "mlp"),
        P("req", "mlp"),
        P("mlp", "req"),
    )
    out_specs = P("req", "mlp", None)
    return jax.shard_map(body, mesh=mesh, in_specs=in_specs, out_specs=out_specs, check_vma=False)
```

```python
import functools

import jax
import jax.numpy as jnp
from jax import lax
from jax.experimental import pallas as pl
from jax.experimental.pallas import tpu as pltpu
from jax.sharding import PartitionSpec as P

HEAD_SIZE = 256
QUERY_HEADS = 6
KEY_VALUE_HEADS = 2


score_scale = 0.0625
negative = -1e30


def lookup(table, index):
    positions = jnp.arange(table.shape[0], dtype=jnp.int32)
    return jnp.sum(jnp.where(positions == index, table, 0))


def rms_rows(attended):
    wide = attended.astype(jnp.float32)
    return (wide * lax.rsqrt(jnp.mean(wide * wide, axis=-1, keepdims=True) + 1e-06)).astype(
        jnp.bfloat16
    )


def wide_body(
    queries,
    cached_key_slots,
    cached_value_slots,
    new_token_keys,
    new_token_values,
    cache_len,
    placing,
    w_gate,
    w_up,
    w_down,
):
    slot_index = lax.axis_index("req")
    mlp_index = lax.axis_index("mlp")
    mlp_count = lax.axis_size("mlp")
    token_inputs = queries.shape[1]
    request_cache = cached_key_slots.shape[1]
    request_new_tokens = new_token_keys.shape[1]
    query_group_width = QUERY_HEADS // KEY_VALUE_HEADS
    row_count = token_inputs // mlp_count
    request = lookup(placing, slot_index)
    live_len = lookup(cache_len, request)
    query_head_rows = queries[0].reshape(
        token_inputs, KEY_VALUE_HEADS, query_group_width, HEAD_SIZE
    )
    request_keys = cached_key_slots[0].reshape(request_cache, KEY_VALUE_HEADS, HEAD_SIZE)
    request_values = cached_value_slots[0].reshape(request_cache, KEY_VALUE_HEADS, HEAD_SIZE)
    new_key_rows = new_token_keys[0].reshape(request_new_tokens, KEY_VALUE_HEADS, HEAD_SIZE)
    new_value_rows = new_token_values[0].reshape(request_new_tokens, KEY_VALUE_HEADS, HEAD_SIZE)
    cache_pos = mlp_index * request_cache + jnp.arange(request_cache, dtype=jnp.int32)
    cache_live = cache_pos < live_len
    scores_old = (
        jnp.einsum(
            "ngrd,cgd->grnc", query_head_rows, request_keys, preferred_element_type=jnp.float32
        )
        * score_scale
    )
    scores_old = jnp.where(cache_live[None, None, None, :], scores_old, negative)
    fresh_pos = mlp_index * request_new_tokens + jnp.arange(request_new_tokens, dtype=jnp.int32)
    causal = fresh_pos[None, :] <= jnp.arange(token_inputs, dtype=jnp.int32)[:, None]
    scores_new = (
        jnp.einsum(
            "ngrd,mgd->grnm", query_head_rows, new_key_rows, preferred_element_type=jnp.float32
        )
        * score_scale
    )
    scores_new = jnp.where(causal[None, None], scores_new, negative)
    local_top = jnp.maximum(scores_old.max(-1), scores_new.max(-1))
    row_top = lax.pmax(local_top, "mlp")
    expo_old = jnp.exp(scores_old - row_top[..., None])
    expo_new = jnp.exp(scores_new - row_top[..., None])
    denom_local = expo_old.sum(-1) + expo_new.sum(-1)
    probs_old = expo_old.astype(jnp.bfloat16)
    probs_new = expo_new.astype(jnp.bfloat16)
    weighted = jnp.einsum(
        "grnc,cgd->ngrd", probs_old, request_values, preferred_element_type=jnp.float32
    )
    weighted = weighted + jnp.einsum(
        "grnm,mgd->ngrd", probs_new, new_value_rows, preferred_element_type=jnp.float32
    )
    weighted, denom = lax.psum((weighted, denom_local), "mlp")
    attended = (
        (weighted / jnp.transpose(denom, (2, 0, 1))[..., None])
        .reshape(token_inputs, QUERY_HEADS * HEAD_SIZE)
        .astype(jnp.bfloat16)
    )
    normed = rms_rows(attended)
    own_attended = lax.dynamic_slice_in_dim(attended, mlp_index * row_count, row_count, 0)
    gate_sum = jnp.dot(
        normed,
        lax.all_gather(w_gate, "req", axis=0, tiled=True),
        preferred_element_type=jnp.float32,
    )
    upper_sum = jnp.dot(
        normed, lax.all_gather(w_up, "req", axis=0, tiled=True), preferred_element_type=jnp.float32
    )
    hidden = (jax.nn.silu(gate_sum) * upper_sum).astype(jnp.bfloat16)
    partial_down = jnp.dot(
        hidden,
        lax.all_gather(w_down, "req", axis=1, tiled=True),
        preferred_element_type=jnp.float32,
    )
    own_rows = lax.psum_scatter(
        partial_down.astype(jnp.bfloat16), "mlp", scatter_dimension=0, tiled=True
    ).astype(jnp.float32)
    residual = own_attended.astype(jnp.float32)
    return (residual + own_rows).astype(jnp.bfloat16)[None]


CHUNKS = 3
KEY_BLOCK = 512
CACHE_PARTS = 4


def other(index, mask, bits):
    flipped = 0
    for b in range(bits):
        flipped = flipped + ((index // (1 << b) + mask // (1 << b)) % 2) * (1 << b)
    return flipped


def settle(ref, sem):
    pltpu.make_async_copy(ref, ref, sem).wait()


def window_kernel(
    cache_len_ref,
    placing_ref,
    queries_ref,
    keys_ref,
    values_ref,
    new_keys_ref,
    new_values_ref,
    gate_ref,
    upper_ref,
    down_ref,
    out_ref,
    weights,
    keys,
    values,
    queries,
    new_keys,
    new_values,
    weighted,
    top,
    denom,
    share_out,
    share_in,
    own_attended,
    normed,
    total,
    pair_out,
    pair_in,
    chain_out,
    chain_in,
    late_out,
    late_in,
    late_pair_out,
    late_pair_in,
    plane_send,
    plane_recv,
    across_send,
    across_recv,
    core_send,
    core_recv,
    own_sem,
    load_sem,
    cache_sem,
    share_send,
    share_recv,
    token_send,
    token_recv,
    pair_send,
    pair_recv,
    chain_send,
    chain_recv,
    late_send,
    late_recv,
    late_pair_send,
    late_pair_recv,
):
    slot = lax.axis_index("req")
    core = lax.axis_index("mlp")
    x, p = slot % 2, slot // 2
    y, z = p % 2, p // 2
    beside = p + 1 - 2 * y
    strip = gate_ref.shape[0]
    width = out_ref.shape[1]
    rows = out_ref.shape[0]
    units = gate_ref.shape[1] // 8
    piece = units // CHUNKS
    chunk = 2 * piece
    group = QUERY_HEADS // KEY_VALUE_HEADS
    tokens = 2 * rows

    def at(place, column):
        return {"req": place * 2 + column, "mlp": core}

    def in_plane(place):
        return at(place, x)

    across = at(p, 1 - x)
    twin = {"req": slot, "mlp": 1 - core}

    def push(source, target, send_sem, recv_sem, device):
        pltpu.make_async_remote_copy(
            src_ref=source,
            dst_ref=target,
            send_sem=send_sem,
            recv_sem=recv_sem,
            device_id=device,
            device_id_type=pl.DeviceIdType.MESH,
        ).start()

    barrier = pltpu.get_barrier_semaphore()
    peers = [in_plane(other(p, k, 3)) for k in range(1, 8)] + [across, twin]
    for peer in peers:
        pl.semaphore_signal(barrier, inc=1, device_id=peer, device_id_type=pl.DeviceIdType.MESH)
    pl.semaphore_wait(barrier, len(peers))

    sources = (gate_ref, upper_ref, down_ref)

    def strip_rows(place, column):
        return pl.ds(pl.multiple_of((place * 2 + column) * strip, 16), strip)

    def piece_columns(j, half):
        return pl.ds(pl.multiple_of(j * chunk + half * piece, 128), piece)

    def source_columns(j, place):
        return pl.ds(pl.multiple_of(place * units + j * piece, 128), piece)

    def issue(j, k):
        place = other(p, k, 3)
        for m in range(3):
            push(
                sources[m].at[:, source_columns(j, place)],
                weights.at[m, strip_rows(p, x), piece_columns(j, core)],
                plane_send.at[j],
                plane_recv.at[j, k],
                in_plane(place),
            )

    def issue_own(j):
        for m in range(3):
            source = sources[m].at[:, source_columns(j, p)]
            target = weights.at[m, strip_rows(p, x), piece_columns(j, core)]
            pltpu.make_async_copy(source, target, own_sem).start()
            push(source, target, across_send, across_recv.at[j, 0], across)
            push(source, target, core_send, core_recv.at[j], twin)

    def block_of(j, k, column):
        return weights.at[:, strip_rows(other(p, k, 3), column), piece_columns(j, core)]

    def relay(j, k):
        block = block_of(j, k, x)
        settle(block, plane_recv.at[j, k])
        push(block, block, across_send, across_recv.at[j, k], across)
        push(block, block, core_send, core_recv.at[j], twin)

    def relay_across(j, k):
        block = block_of(j, k, 1 - x)
        settle(block, across_recv.at[j, k])
        push(block, block, core_send, core_recv.at[j], twin)

    def chunk_done(j):
        settle(weights.at[:, :, piece_columns(j, 1 - core)], core_recv.at[j])

    far = [(j, k) for j in range(CHUNKS) for k in (4, 5, 6, 7)]
    near = [(j, k) for j in range(CHUNKS) for k in (1, 2, 3)]

    issue(*near[2])
    issue(*far[5])
    issue(*far[0])

    part = keys_ref.shape[0] // CACHE_PARTS
    pltpu.make_async_copy(queries_ref, queries, load_sem.at[0]).start()
    pltpu.make_async_copy(new_keys_ref, new_keys, load_sem.at[1]).start()
    pltpu.make_async_copy(new_values_ref, new_values, load_sem.at[2]).start()
    for n in range(CACHE_PARTS):
        span = pl.ds(n * part, part)
        pltpu.make_async_copy(keys_ref.at[span], keys.at[span], cache_sem.at[0, n]).start()
        pltpu.make_async_copy(values_ref.at[span], values.at[span], cache_sem.at[1, n]).start()
    live_len = cache_len_ref[placing_ref[slot]]
    settle(queries, load_sem.at[0])
    settle(new_keys, load_sem.at[1])
    settle(new_values, load_sem.at[2])
    queries[...] = queries[...] * jnp.bfloat16(score_scale)

    def against(a, b):
        return lax.dot_general(
            a, b, (((1,), (1,)), ((), ())), preferred_element_type=jnp.float32
        )

    def lanes(h, size):
        return pl.ds(pl.multiple_of(h * size, 128), size)

    def spread(narrow, size):
        return jnp.concatenate([narrow] * (size // 128), axis=1)

    def folded(wide_rows):
        parts = [wide_rows[:, n : n + 128] for n in range(0, wide_rows.shape[1], 128)]
        while len(parts) > 1:
            parts = [parts[n] + parts[n + 1] for n in range(0, len(parts), 2)]
        return parts[0]

    fresh_pos = core * rows + lax.broadcasted_iota(jnp.int32, (tokens, rows), 1)
    causal = fresh_pos <= lax.broadcasted_iota(jnp.int32, (tokens, rows), 0)
    for h in range(QUERY_HEADS):
        g = h // group
        head = queries[:, h * HEAD_SIZE : (h + 1) * HEAD_SIZE]
        scores = against(head, new_keys[:, g * HEAD_SIZE : (g + 1) * HEAD_SIZE])
        scores = jnp.where(causal, scores, negative)
        row_top = jnp.broadcast_to(jnp.max(scores, axis=1, keepdims=True), (tokens, 128))
        expo = jnp.exp(scores - spread(row_top, rows))
        top[h] = row_top
        denom[h] = folded(expo)
        weighted[h] = jnp.dot(
            expo.astype(jnp.bfloat16),
            new_values[:, g * HEAD_SIZE : (g + 1) * HEAD_SIZE],
            preferred_element_type=jnp.float32,
        )

    def attend_block(g, start):
        span = pl.ds(pl.multiple_of(start, KEY_BLOCK), KEY_BLOCK)
        block_keys = keys[span, lanes(g, HEAD_SIZE)]
        block_values = values[span, lanes(g, HEAD_SIZE)]
        cache_pos = core * keys.shape[0] + start
        live = cache_pos + lax.broadcasted_iota(jnp.int32, (1, KEY_BLOCK), 1) < live_len
        for n in range(group):
            h = g * group + n
            scores = against(queries[:, lanes(h, HEAD_SIZE)], block_keys)
            scores = jnp.where(live, scores, negative)
            old_top = top[h]
            row_top = jnp.maximum(old_top, jnp.max(scores, axis=1, keepdims=True))
            fade = jnp.exp(old_top - row_top)
            expo = jnp.exp(scores - spread(row_top, KEY_BLOCK))
            top[h] = row_top
            denom[h] = denom[h] * fade + folded(expo)
            weighted[h] = weighted[h] * spread(fade, HEAD_SIZE) + jnp.dot(
                expo.astype(jnp.bfloat16), block_values, preferred_element_type=jnp.float32
            )

    def share(h):
        away = pl.ds(pl.multiple_of((1 - core) * rows, rows), rows)
        share_out[h, :, :HEAD_SIZE] = weighted[h, away, :]
        share_out[h, :, HEAD_SIZE : HEAD_SIZE + 128] = top[h, away, :]
        share_out[h, :, HEAD_SIZE + 128 :] = denom[h, away, :]
        push(share_out.at[h], share_in.at[h], share_send, share_recv, twin)

    steps = KEY_VALUE_HEADS * CACHE_PARTS
    def after_0():
        issue(*far[4])
        for j in range(CHUNKS):
            issue_own(j)

    def after_1():
        relay(*near[2])

    def after_2():
        issue(*near[6])
        issue(*near[4])

    def after_3():
        issue(*far[1])
        issue(*near[7])

    def after_5():
        issue(*far[3])
        relay(*near[6])

    def after_6():
        issue(*near[8])
        relay(*near[7])
        issue(*near[5])
        relay(*far[0])
        issue(*far[10])
        relay_across(2, 0)
        relay(*far[4])
        relay_across(*far[0])
        relay(*near[4])
        relay_across(0, 3)

    def after_7():
        issue(*far[7])
        relay(*far[1])
        relay(*far[5])
        relay_across(*far[4])
        relay(*far[3])
        issue(*near[3])
        issue(*near[1])

    plan = {0: after_0, 1: after_1, 2: after_2, 3: after_3, 5: after_5, 6: after_6, 7: after_7}

    def attend_step(s, carry):
        g, n = s // CACHE_PARTS, s % CACHE_PARTS

        @pl.when(s < CACHE_PARTS)
        def _():
            span = pl.ds(pl.multiple_of(n * part, part), part)
            settle(keys.at[span], cache_sem.at[0, n])
            settle(values.at[span], cache_sem.at[1, n])

        def inner(i, c):
            attend_block(g, n * part + i * KEY_BLOCK)
            return c

        lax.fori_loop(0, part // KEY_BLOCK, inner, 0)

        @pl.when(n == CACHE_PARTS - 1)
        def _():
            for i in range(group):
                share(g * group + i)

        for step, events in plan.items():
            pl.when(s == step)(events)

        return carry

    lax.fori_loop(0, steps, attend_step, 0)

    settle(share_in, share_recv)
    mine = pl.ds(pl.multiple_of(core * rows, rows), rows)
    squares = jnp.zeros((rows, 128), jnp.float32)
    for h in range(QUERY_HEADS):
        own_top, peer_top = top[h, mine, :], share_in[h, :, HEAD_SIZE : HEAD_SIZE + 128]
        row_top = jnp.maximum(own_top, peer_top)
        own_scale, peer_scale = jnp.exp(own_top - row_top), jnp.exp(peer_top - row_top)
        lane_sums = denom[h, mine, :] * own_scale + share_in[h, :, HEAD_SIZE + 128 :] * peer_scale
        head = weighted[h, mine, :] * spread(own_scale, HEAD_SIZE)
        head = head + share_in[h, :, :HEAD_SIZE] * spread(peer_scale, HEAD_SIZE)
        head = (head / jnp.sum(lane_sums, axis=1, keepdims=True)).astype(jnp.bfloat16)
        own_attended[:, h * HEAD_SIZE : (h + 1) * HEAD_SIZE] = head
        wide = head.astype(jnp.float32)
        squares = squares + folded(wide * wide)
    scale = lax.rsqrt(jnp.sum(squares, axis=1, keepdims=True) / width + 1e-06)

    def token_rows(place, count=1):
        return pl.ds(pl.multiple_of(place * rows, rows), count * rows)

    normed[token_rows(p), :] = (own_attended[...].astype(jnp.float32) * scale).astype(jnp.bfloat16)

    def pass_on(place, way, d, device):
        block = normed.at[token_rows(place)]
        push(block, block, token_send.at[way, d], token_recv.at[place], device)

    def sent(place, way, d):
        settle(normed.at[token_rows(place)], token_send.at[way, d])

    def spread_tokens(d):
        below, above = p - 2 * d, p + 2 * d
        if d == 0:
            pl.when(z < 3)(lambda: pass_on(p, 1, 0, in_plane(p + 2)))
            pl.when(z > 0)(lambda: pass_on(p, 2, 0, in_plane(p - 2)))
            pass_on(p, 0, 0, in_plane(beside))
            return

        @pl.when(z >= d)
        def _():
            settle(normed.at[token_rows(below)], token_recv.at[below])
            pl.when(z < 3)(lambda: pass_on(below, 1, d, in_plane(p + 2)))
            pass_on(below, 0, d, in_plane(beside))

        @pl.when(z + d <= 3)
        def _():
            settle(normed.at[token_rows(above)], token_recv.at[above])
            pl.when(z > 0)(lambda: pass_on(above, 2, d, in_plane(p - 2)))
            pass_on(above, 0, 3 + d, in_plane(beside))

    def tokens_sent():
        sent(p, 0, 0)
        pl.when(z < 3)(lambda: sent(p, 1, 0))
        pl.when(z > 0)(lambda: sent(p, 2, 0))
        for d in range(1, 4):
            below, above = p - 2 * d, p + 2 * d
            pl.when(z >= d)(functools.partial(sent, below, 0, d))
            pl.when((z >= d) & (z < 3))(functools.partial(sent, below, 1, d))
            pl.when(z + d <= 3)(functools.partial(sent, above, 0, 3 + d))
            pl.when((z + d <= 3) & (z > 0))(functools.partial(sent, above, 2, d))

    def tokens_here():
        for plane in range(4):
            place = plane * 2 + 1 - y
            settle(normed.at[token_rows(place)], token_recv.at[place])

    def mix(j, span):
        columns = pl.ds(j * chunk, chunk)
        inputs = normed[span, :]
        gate_sum = jnp.dot(inputs, weights[0, :, columns], preferred_element_type=jnp.float32)
        upper_sum = jnp.dot(inputs, weights[1, :, columns], preferred_element_type=jnp.float32)
        hidden = (gate_sum / (1.0 + jnp.exp(-gate_sum)) * upper_sum).astype(jnp.bfloat16)
        return against(hidden, weights[2, :, columns])

    half_rows = 4 * rows

    def early(j, half):
        span = pl.ds(half * half_rows, half_rows)
        if j == 0:
            total[span, :] = mix(j, span)
        else:
            total[span, :] += mix(j, span)

    spread_tokens(0)
    relay(*near[3])
    relay(*near[8])
    issue(*near[0])
    relay(*near[1])
    spread_tokens(1)
    spread_tokens(2)
    relay(*near[0])
    relay_across(1, 1)
    issue(*far[2])
    relay_across(2, 2)
    relay(*far[7])
    relay_across(0, 1)
    relay_across(*far[3])
    relay(*near[5])
    relay(*far[10])
    issue(*far[9])
    relay(*far[2])
    relay_across(1, 2)
    issue(*far[6])
    relay_across(2, 1)
    relay_across(*far[5])
    spread_tokens(3)
    relay_across(0, 2)
    relay_across(*far[7])
    relay_across(*far[2])
    relay_across(2, 3)
    issue(*far[8])
    relay(*far[9])
    relay_across(*far[10])
    relay_across(*far[1])
    relay_across(0, 0)
    settle(weights.at[:, pl.ds(0, strip), pl.ds(0, units)], own_sem)
    chunk_done(0)
    relay(*far[6])
    relay_across(1, 0)
    tokens_here()
    relay(*far[8])
    issue(*far[11])
    early(0, 0)
    relay_across(1, 3)
    relay_across(*far[6])
    early(0, 1)
    chunk_done(1)
    relay(*far[11])
    early(1, 0)
    early(1, 1)
    relay_across(*far[9])
    relay_across(*far[8])
    relay_across(*far[11])
    chunk_done(2)

    upper_half = z // 2
    folded_z = z + upper_half * (3 - 2 * z)

    def plane_of(i):
        base = (3, 2, 1 - folded_z, folded_z)[i]
        return base + upper_half * (3 - 2 * base)

    front = pair_out.shape[2]
    early_lanes, late_lanes = pl.ds(0, front), pl.ds(front, width - front)

    def last(i):
        plane = plane_of(i)
        span = token_rows(plane * 2, 2)
        total[span, :] += mix(CHUNKS - 1, span)
        away = token_rows(plane * 2 + 1 - y)
        pair_out[i] = total[away, early_lanes].astype(jnp.bfloat16)
        push(pair_out.at[i], pair_in.at[i], pair_send.at[i], pair_recv.at[i], in_plane(beside))

    def column_sum(i):
        settle(pair_in.at[i], pair_recv.at[i])
        own = token_rows(plane_of(i) * 2 + y)
        total[own, early_lanes] += pair_in[i].astype(jnp.float32)
        return own

    def add_early(span, way, plane):
        settle(chain_in.at[way, plane], chain_recv.at[way, plane])
        total[span, early_lanes] += chain_in[way, plane].astype(jnp.float32)

    def add_late(span, way, plane):
        settle(late_in.at[way, plane], late_recv.at[way, plane])
        total[span, late_lanes] += late_in[way, plane].astype(jnp.float32)

    def onward(i, span, lanes_of, add, out, into, send_sem, recv_sem):
        plane = plane_of(i)

        def go(way, device, has_more):
            @pl.when(has_more)
            def _():
                add(span, way, plane)

            out[i] = total[span, lanes_of].astype(jnp.bfloat16)
            push(out.at[i], into.at[way, plane], send_sem.at[i], recv_sem.at[way, plane], device)

        pl.when(plane > z)(lambda: go(0, in_plane(p + 2), z > 0))
        pl.when(plane < z)(lambda: go(1, in_plane(p - 2), z < 3))

    def along(i):
        own = column_sum(i)
        onward(i, own, early_lanes, add_early, chain_out, chain_in, chain_send, chain_recv)

    def along_late(i):
        span = token_rows(plane_of(i) * 2, 2)
        onward(i, span, late_lanes, add_late, late_out, late_in, late_send, late_recv)

    def settle_late():
        span = token_rows(z * 2, 2)
        pl.when(z > 0)(lambda: add_late(span, 0, z))
        pl.when(z < 3)(lambda: add_late(span, 1, z))
        late_pair_out[...] = total[token_rows(beside), late_lanes].astype(jnp.bfloat16)
        push(late_pair_out, late_pair_in, late_pair_send, late_pair_recv, in_plane(beside))

    last(0)
    last(1)
    along_late(0)
    last(2)
    along_late(1)
    last(3)
    along_late(2)
    along(0)
    along(1)
    settle_late()
    along(2)
    own = column_sum(3)
    pl.when(z > 0)(lambda: add_early(own, 0, z))
    pl.when(z < 3)(lambda: add_early(own, 1, z))
    settle(late_pair_in, late_pair_recv)
    total[own, late_lanes] += late_pair_in[...].astype(jnp.float32)
    out_ref[...] = (own_attended[...].astype(jnp.float32) + total[own, :]).astype(jnp.bfloat16)

    for j in range(CHUNKS):
        settle(weights.at[:, pl.ds(0, 7 * strip), pl.ds(0, piece)], plane_send.at[j])
    settle(weights.at[:, pl.ds(0, 8 * strip), pl.ds(0, units)], across_send)
    settle(weights.at[:, :, pl.ds(0, units)], core_send)
    settle(share_out, share_send)
    tokens_sent()
    for i in range(4):
        settle(pair_out.at[i], pair_send.at[i])
    for i in range(3):
        settle(chain_out.at[i], chain_send.at[i])
        settle(late_out.at[i], late_send.at[i])
    settle(late_pair_out, late_pair_send)


def window(
    queries,
    cached_key_slots,
    cached_value_slots,
    new_token_keys,
    new_token_values,
    cache_len,
    placing,
    w_gate,
    w_up,
    w_down,
):
    tokens, width = queries.shape
    rows = tokens // 2
    bf16, f32 = jnp.bfloat16, jnp.float32
    vmem, dma = pltpu.VMEM, pltpu.SemaphoreType.DMA
    hidden_units = w_gate.shape[1] // 4
    late = width // 6
    scalars = pl.BlockSpec(memory_space=pltpu.SMEM)
    return pl.pallas_call(
        window_kernel,
        out_shape=jax.ShapeDtypeStruct((rows, width), bf16),
        in_specs=[scalars] * 2 + [pl.BlockSpec(memory_space=pl.ANY)] * 8,
        out_specs=pl.BlockSpec(memory_space=pltpu.VMEM),
        scratch_shapes=[
            vmem((3, width, hidden_units), bf16),
            vmem(cached_key_slots.shape, bf16),
            vmem(cached_value_slots.shape, bf16),
            vmem((tokens, width), bf16),
            vmem(new_token_keys.shape, bf16),
            vmem(new_token_values.shape, bf16),
            vmem((QUERY_HEADS, tokens, HEAD_SIZE), f32),
            vmem((QUERY_HEADS, tokens, 128), f32),
            vmem((QUERY_HEADS, tokens, 128), f32),
            vmem((QUERY_HEADS, rows, 2 * HEAD_SIZE), f32),
            vmem((QUERY_HEADS, rows, 2 * HEAD_SIZE), f32),
            vmem((rows, width), bf16),
            vmem((8 * rows, width), bf16),
            vmem((8 * rows, width), f32),
            vmem((4, rows, width - late), bf16),
            vmem((4, rows, width - late), bf16),
            vmem((3, rows, width - late), bf16),
            vmem((2, 4, rows, width - late), bf16),
            vmem((3, tokens, late), bf16),
            vmem((2, 4, tokens, late), bf16),
            vmem((rows, late), bf16),
            vmem((rows, late), bf16),
            dma((CHUNKS,)),
            dma((CHUNKS, 8)),
            dma,
            dma((CHUNKS, 8)),
            dma,
            dma((CHUNKS,)),
            dma,
            dma((3,)),
            dma((2, CACHE_PARTS)),
            dma,
            dma,
            dma((3, 7)),
            dma((8,)),
            dma((4,)),
            dma((4,)),
            dma((3,)),
            dma((2, 4)),
            dma((3,)),
            dma((2, 4)),
            dma,
            dma,
        ],
        compiler_params=pltpu.CompilerParams(
            collective_id=0, has_side_effects=True, vmem_limit_bytes=60 * 1024 * 1024
        ),
        name="window",
    )(
        cache_len,
        placing,
        queries,
        cached_key_slots,
        cached_value_slots,
        new_token_keys,
        new_token_values,
        w_gate,
        w_up,
        w_down.T,
    )


def body(
    queries,
    cached_key_slots,
    cached_value_slots,
    new_token_keys,
    new_token_values,
    cache_len,
    placing,
    w_gate,
    w_up,
    w_down,
):
    if lax.axis_size("req") != 16 or lax.axis_size("mlp") != 2:
        return wide_body(
            queries,
            cached_key_slots,
            cached_value_slots,
            new_token_keys,
            new_token_values,
            cache_len,
            placing,
            w_gate,
            w_up,
            w_down,
        )
    return window(
        queries[0],
        cached_key_slots[0],
        cached_value_slots[0],
        new_token_keys[0],
        new_token_values[0],
        cache_len,
        placing,
        w_gate,
        w_up,
        w_down,
    )[None]


def solution(mesh):
    in_specs = (
        P("req", None, None),
        P("req", "mlp", None),
        P("req", "mlp", None),
        P("req", "mlp", None),
        P("req", "mlp", None),
        P(),
        P(),
        P("req", "mlp"),
        P("req", "mlp"),
        P("mlp", "req"),
    )
    out_specs = P("req", "mlp", None)
    return jax.shard_map(body, mesh=mesh, in_specs=in_specs, out_specs=out_specs, check_vma=False)
```

```python
import functools

import jax
import jax.numpy as jnp
from jax import lax
from jax.experimental import pallas as pl
from jax.experimental.pallas import tpu as pltpu
from jax.sharding import PartitionSpec as P

HEAD_SIZE = 256
QUERY_HEADS = 6
KEY_VALUE_HEADS = 2


score_scale = 0.0625
negative = -1e30


def lookup(table, index):
    positions = jnp.arange(table.shape[0], dtype=jnp.int32)
    return jnp.sum(jnp.where(positions == index, table, 0))


def rms_rows(attended):
    wide = attended.astype(jnp.float32)
    return (wide * lax.rsqrt(jnp.mean(wide * wide, axis=-1, keepdims=True) + 1e-06)).astype(
        jnp.bfloat16
    )


def wide_body(
    queries,
    cached_key_slots,
    cached_value_slots,
    new_token_keys,
    new_token_values,
    cache_len,
    placing,
    w_gate,
    w_up,
    w_down,
):
    slot_index = lax.axis_index("req")
    mlp_index = lax.axis_index("mlp")
    mlp_count = lax.axis_size("mlp")
    token_inputs = queries.shape[1]
    request_cache = cached_key_slots.shape[1]
    request_new_tokens = new_token_keys.shape[1]
    query_group_width = QUERY_HEADS // KEY_VALUE_HEADS
    row_count = token_inputs // mlp_count
    request = lookup(placing, slot_index)
    live_len = lookup(cache_len, request)
    query_head_rows = queries[0].reshape(
        token_inputs, KEY_VALUE_HEADS, query_group_width, HEAD_SIZE
    )
    request_keys = cached_key_slots[0].reshape(request_cache, KEY_VALUE_HEADS, HEAD_SIZE)
    request_values = cached_value_slots[0].reshape(request_cache, KEY_VALUE_HEADS, HEAD_SIZE)
    new_key_rows = new_token_keys[0].reshape(request_new_tokens, KEY_VALUE_HEADS, HEAD_SIZE)
    new_value_rows = new_token_values[0].reshape(request_new_tokens, KEY_VALUE_HEADS, HEAD_SIZE)
    cache_pos = mlp_index * request_cache + jnp.arange(request_cache, dtype=jnp.int32)
    cache_live = cache_pos < live_len
    scores_old = (
        jnp.einsum(
            "ngrd,cgd->grnc", query_head_rows, request_keys, preferred_element_type=jnp.float32
        )
        * score_scale
    )
    scores_old = jnp.where(cache_live[None, None, None, :], scores_old, negative)
    fresh_pos = mlp_index * request_new_tokens + jnp.arange(request_new_tokens, dtype=jnp.int32)
    causal = fresh_pos[None, :] <= jnp.arange(token_inputs, dtype=jnp.int32)[:, None]
    scores_new = (
        jnp.einsum(
            "ngrd,mgd->grnm", query_head_rows, new_key_rows, preferred_element_type=jnp.float32
        )
        * score_scale
    )
    scores_new = jnp.where(causal[None, None], scores_new, negative)
    local_top = jnp.maximum(scores_old.max(-1), scores_new.max(-1))
    row_top = lax.pmax(local_top, "mlp")
    expo_old = jnp.exp(scores_old - row_top[..., None])
    expo_new = jnp.exp(scores_new - row_top[..., None])
    denom_local = expo_old.sum(-1) + expo_new.sum(-1)
    probs_old = expo_old.astype(jnp.bfloat16)
    probs_new = expo_new.astype(jnp.bfloat16)
    weighted = jnp.einsum(
        "grnc,cgd->ngrd", probs_old, request_values, preferred_element_type=jnp.float32
    )
    weighted = weighted + jnp.einsum(
        "grnm,mgd->ngrd", probs_new, new_value_rows, preferred_element_type=jnp.float32
    )
    weighted, denom = lax.psum((weighted, denom_local), "mlp")
    attended = (
        (weighted / jnp.transpose(denom, (2, 0, 1))[..., None])
        .reshape(token_inputs, QUERY_HEADS * HEAD_SIZE)
        .astype(jnp.bfloat16)
    )
    normed = rms_rows(attended)
    own_attended = lax.dynamic_slice_in_dim(attended, mlp_index * row_count, row_count, 0)
    gate_sum = jnp.dot(
        normed,
        lax.all_gather(w_gate, "req", axis=0, tiled=True),
        preferred_element_type=jnp.float32,
    )
    upper_sum = jnp.dot(
        normed, lax.all_gather(w_up, "req", axis=0, tiled=True), preferred_element_type=jnp.float32
    )
    hidden = (jax.nn.silu(gate_sum) * upper_sum).astype(jnp.bfloat16)
    partial_down = jnp.dot(
        hidden,
        lax.all_gather(w_down, "req", axis=1, tiled=True),
        preferred_element_type=jnp.float32,
    )
    own_rows = lax.psum_scatter(
        partial_down.astype(jnp.bfloat16), "mlp", scatter_dimension=0, tiled=True
    ).astype(jnp.float32)
    residual = own_attended.astype(jnp.float32)
    return (residual + own_rows).astype(jnp.bfloat16)[None]


CHUNKS = 3
KEY_BLOCK = 512
CACHE_PARTS = 4


def other(index, mask, bits):
    flipped = 0
    for b in range(bits):
        flipped = flipped + ((index // (1 << b) + mask // (1 << b)) % 2) * (1 << b)
    return flipped


def settle(ref, sem):
    pltpu.make_async_copy(ref, ref, sem).wait()


def window_kernel(
    cache_len_ref,
    placing_ref,
    queries_ref,
    keys_ref,
    values_ref,
    new_keys_ref,
    new_values_ref,
    gate_ref,
    upper_ref,
    down_ref,
    out_ref,
    weights,
    keys,
    values,
    queries,
    new_keys,
    new_values,
    weighted,
    top,
    denom,
    share_out,
    share_in,
    own_attended,
    normed,
    total,
    pair_out,
    pair_in,
    chain_out,
    chain_in,
    late_out,
    late_in,
    late_pair_out,
    late_pair_in,
    plane_send,
    plane_recv,
    across_send,
    across_recv,
    core_send,
    core_recv,
    own_sem,
    load_sem,
    cache_sem,
    share_send,
    share_recv,
    token_send,
    token_recv,
    pair_send,
    pair_recv,
    chain_send,
    chain_recv,
    late_send,
    late_recv,
    late_pair_send,
    late_pair_recv,
):
    slot = lax.axis_index("req")
    core = lax.axis_index("mlp")
    x, p = slot % 2, slot // 2
    y, z = p % 2, p // 2
    beside = p + 1 - 2 * y
    strip = gate_ref.shape[0]
    width = out_ref.shape[1]
    rows = out_ref.shape[0]
    units = gate_ref.shape[1] // 8
    piece = units // CHUNKS
    chunk = 2 * piece
    group = QUERY_HEADS // KEY_VALUE_HEADS
    tokens = 2 * rows

    def at(place, column):
        return {"req": place * 2 + column, "mlp": core}

    def in_plane(place):
        return at(place, x)

    across = at(p, 1 - x)
    twin = {"req": slot, "mlp": 1 - core}

    def push(source, target, send_sem, recv_sem, device):
        pltpu.make_async_remote_copy(
            src_ref=source,
            dst_ref=target,
            send_sem=send_sem,
            recv_sem=recv_sem,
            device_id=device,
            device_id_type=pl.DeviceIdType.MESH,
        ).start()

    barrier = pltpu.get_barrier_semaphore()
    peers = [in_plane(other(p, k, 3)) for k in range(1, 8)] + [across, twin]
    for peer in peers:
        pl.semaphore_signal(barrier, inc=1, device_id=peer, device_id_type=pl.DeviceIdType.MESH)
    pl.semaphore_wait(barrier, len(peers))

    sources = (gate_ref, upper_ref, down_ref)

    def strip_rows(place, column):
        return pl.ds(pl.multiple_of((place * 2 + column) * strip, 16), strip)

    def piece_columns(j, half):
        return pl.ds(pl.multiple_of(j * chunk + half * piece, 128), piece)

    def source_columns(j, place):
        return pl.ds(pl.multiple_of(place * units + j * piece, 128), piece)

    def issue(j, k):
        place = other(p, k, 3)
        for m in range(3):
            push(
                sources[m].at[:, source_columns(j, place)],
                weights.at[m, strip_rows(p, x), piece_columns(j, core)],
                plane_send.at[j],
                plane_recv.at[j, k],
                in_plane(place),
            )

    def issue_own(j):
        for m in range(3):
            source = sources[m].at[:, source_columns(j, p)]
            target = weights.at[m, strip_rows(p, x), piece_columns(j, core)]
            pltpu.make_async_copy(source, target, own_sem).start()
            push(source, target, across_send, across_recv.at[j, 0], across)
            push(source, target, core_send, core_recv.at[j], twin)

    def block_of(j, k, column):
        return weights.at[:, strip_rows(other(p, k, 3), column), piece_columns(j, core)]

    def relay(j, k):
        block = block_of(j, k, x)
        settle(block, plane_recv.at[j, k])
        push(block, block, across_send, across_recv.at[j, k], across)
        push(block, block, core_send, core_recv.at[j], twin)

    def relay_across(j, k):
        block = block_of(j, k, 1 - x)
        settle(block, across_recv.at[j, k])
        push(block, block, core_send, core_recv.at[j], twin)

    def chunk_done(j):
        settle(weights.at[:, :, piece_columns(j, 1 - core)], core_recv.at[j])

    far = [(j, k) for j in range(CHUNKS) for k in (4, 5, 6, 7)]
    near = [(j, k) for j in range(CHUNKS) for k in (1, 2, 3)]

    issue(*near[2])
    issue(*far[5])
    issue(*far[0])

    part = keys_ref.shape[0] // CACHE_PARTS
    pltpu.make_async_copy(queries_ref, queries, load_sem.at[0]).start()
    pltpu.make_async_copy(new_keys_ref, new_keys, load_sem.at[1]).start()
    pltpu.make_async_copy(new_values_ref, new_values, load_sem.at[2]).start()
    for n in range(CACHE_PARTS):
        span = pl.ds(n * part, part)
        pltpu.make_async_copy(keys_ref.at[span], keys.at[span], cache_sem.at[0, n]).start()
        pltpu.make_async_copy(values_ref.at[span], values.at[span], cache_sem.at[1, n]).start()
    live_len = cache_len_ref[placing_ref[slot]]
    settle(queries, load_sem.at[0])
    settle(new_keys, load_sem.at[1])
    settle(new_values, load_sem.at[2])
    queries[...] = queries[...] * jnp.bfloat16(score_scale)

    def against(a, b):
        return lax.dot_general(
            a, b, (((1,), (1,)), ((), ())), preferred_element_type=jnp.float32
        )

    def lanes(h, size):
        return pl.ds(pl.multiple_of(h * size, 128), size)

    def spread(narrow, size):
        return jnp.concatenate([narrow] * (size // 128), axis=1)

    def folded(wide_rows):
        parts = [wide_rows[:, n : n + 128] for n in range(0, wide_rows.shape[1], 128)]
        while len(parts) > 1:
            parts = [parts[n] + parts[n + 1] for n in range(0, len(parts), 2)]
        return parts[0]

    fresh_pos = core * rows + lax.broadcasted_iota(jnp.int32, (tokens, rows), 1)
    causal = fresh_pos <= lax.broadcasted_iota(jnp.int32, (tokens, rows), 0)
    for h in range(QUERY_HEADS):
        g = h // group
        head = queries[:, h * HEAD_SIZE : (h + 1) * HEAD_SIZE]
        scores = against(head, new_keys[:, g * HEAD_SIZE : (g + 1) * HEAD_SIZE])
        scores = jnp.where(causal, scores, negative)
        row_top = jnp.broadcast_to(jnp.max(scores, axis=1, keepdims=True), (tokens, 128))
        expo = jnp.exp(scores - spread(row_top, rows))
        top[h] = row_top
        denom[h] = folded(expo)
        weighted[h] = jnp.dot(
            expo.astype(jnp.bfloat16),
            new_values[:, g * HEAD_SIZE : (g + 1) * HEAD_SIZE],
            preferred_element_type=jnp.float32,
        )

    def attend_block(g, start):
        span = pl.ds(pl.multiple_of(start, KEY_BLOCK), KEY_BLOCK)
        block_keys = keys[span, lanes(g, HEAD_SIZE)]
        block_values = values[span, lanes(g, HEAD_SIZE)]
        cache_pos = core * keys.shape[0] + start
        live = cache_pos + lax.broadcasted_iota(jnp.int32, (1, KEY_BLOCK), 1) < live_len
        for n in range(group):
            h = g * group + n
            scores = against(queries[:, lanes(h, HEAD_SIZE)], block_keys)
            scores = jnp.where(live, scores, negative)
            old_top = top[h]
            row_top = jnp.maximum(old_top, jnp.max(scores, axis=1, keepdims=True))
            fade = jnp.exp(old_top - row_top)
            expo = jnp.exp(scores - spread(row_top, KEY_BLOCK))
            top[h] = row_top
            denom[h] = denom[h] * fade + folded(expo)
            weighted[h] = weighted[h] * spread(fade, HEAD_SIZE) + jnp.dot(
                expo.astype(jnp.bfloat16), block_values, preferred_element_type=jnp.float32
            )

    def share(h):
        away = pl.ds(pl.multiple_of((1 - core) * rows, rows), rows)
        share_out[h, :, :HEAD_SIZE] = weighted[h, away, :]
        share_out[h, :, HEAD_SIZE : HEAD_SIZE + 128] = top[h, away, :]
        share_out[h, :, HEAD_SIZE + 128 :] = denom[h, away, :]
        push(share_out.at[h], share_in.at[h], share_send, share_recv, twin)

    steps = KEY_VALUE_HEADS * CACHE_PARTS
    def after_0():
        issue(*far[4])
        for j in range(CHUNKS):
            issue_own(j)

    def after_1():
        relay(*near[2])

    def after_2():
        issue(*near[6])
        issue(*near[4])

    def after_3():
        issue(*far[1])
        issue(*near[7])

    def after_5():
        issue(*far[3])
        relay(*near[6])

    def after_6():
        issue(*near[8])
        relay(*near[7])
        issue(*near[5])
        relay(*far[0])
        issue(*far[10])
        relay_across(2, 0)
        relay(*far[4])
        relay_across(*far[0])
        relay(*near[4])
        relay_across(0, 3)

    def after_7():
        issue(*far[7])
        relay(*far[1])
        relay(*far[5])
        relay_across(*far[4])
        relay(*far[3])
        issue(*near[3])
        issue(*near[1])

    plan = {0: after_0, 1: after_1, 2: after_2, 3: after_3, 5: after_5, 6: after_6, 7: after_7}

    def attend_step(s, carry):
        g, n = s // CACHE_PARTS, s % CACHE_PARTS

        @pl.when(s < CACHE_PARTS)
        def _():
            span = pl.ds(pl.multiple_of(n * part, part), part)
            settle(keys.at[span], cache_sem.at[0, n])
            settle(values.at[span], cache_sem.at[1, n])

        def inner(i, c):
            attend_block(g, n * part + i * KEY_BLOCK)
            return c

        lax.fori_loop(0, part // KEY_BLOCK, inner, 0)

        @pl.when(n == CACHE_PARTS - 1)
        def _():
            for i in range(group):
                share(g * group + i)

        for step, events in plan.items():
            pl.when(s == step)(events)

        return carry

    lax.fori_loop(0, steps, attend_step, 0)

    settle(share_in, share_recv)
    mine = pl.ds(pl.multiple_of(core * rows, rows), rows)
    squares = jnp.zeros((rows, 128), jnp.float32)
    for h in range(QUERY_HEADS):
        own_top, peer_top = top[h, mine, :], share_in[h, :, HEAD_SIZE : HEAD_SIZE + 128]
        row_top = jnp.maximum(own_top, peer_top)
        own_scale, peer_scale = jnp.exp(own_top - row_top), jnp.exp(peer_top - row_top)
        lane_sums = denom[h, mine, :] * own_scale + share_in[h, :, HEAD_SIZE + 128 :] * peer_scale
        head = weighted[h, mine, :] * spread(own_scale, HEAD_SIZE)
        head = head + share_in[h, :, :HEAD_SIZE] * spread(peer_scale, HEAD_SIZE)
        head = (head / jnp.sum(lane_sums, axis=1, keepdims=True)).astype(jnp.bfloat16)
        own_attended[:, h * HEAD_SIZE : (h + 1) * HEAD_SIZE] = head
        wide = head.astype(jnp.float32)
        squares = squares + folded(wide * wide)
    scale = lax.rsqrt(jnp.sum(squares, axis=1, keepdims=True) / width + 1e-06)

    def token_rows(place, count=1):
        return pl.ds(pl.multiple_of(place * rows, rows), count * rows)

    normed[token_rows(p), :] = (own_attended[...].astype(jnp.float32) * scale).astype(jnp.bfloat16)

    def pass_on(place, way, d, device):
        block = normed.at[token_rows(place)]
        push(block, block, token_send.at[way, d], token_recv.at[place], device)

    def sent(place, way, d):
        settle(normed.at[token_rows(place)], token_send.at[way, d])

    def spread_tokens(d):
        below, above = p - 2 * d, p + 2 * d
        if d == 0:
            pl.when(z < 3)(lambda: pass_on(p, 1, 0, in_plane(p + 2)))
            pl.when(z > 0)(lambda: pass_on(p, 2, 0, in_plane(p - 2)))
            pass_on(p, 0, 0, in_plane(beside))
            return

        @pl.when(z >= d)
        def _():
            settle(normed.at[token_rows(below)], token_recv.at[below])
            pl.when(z < 3)(lambda: pass_on(below, 1, d, in_plane(p + 2)))
            pass_on(below, 0, d, in_plane(beside))

        @pl.when(z + d <= 3)
        def _():
            settle(normed.at[token_rows(above)], token_recv.at[above])
            pl.when(z > 0)(lambda: pass_on(above, 2, d, in_plane(p - 2)))
            pass_on(above, 0, 3 + d, in_plane(beside))

    def tokens_sent():
        sent(p, 0, 0)
        pl.when(z < 3)(lambda: sent(p, 1, 0))
        pl.when(z > 0)(lambda: sent(p, 2, 0))
        for d in range(1, 4):
            below, above = p - 2 * d, p + 2 * d
            pl.when(z >= d)(functools.partial(sent, below, 0, d))
            pl.when((z >= d) & (z < 3))(functools.partial(sent, below, 1, d))
            pl.when(z + d <= 3)(functools.partial(sent, above, 0, 3 + d))
            pl.when((z + d <= 3) & (z > 0))(functools.partial(sent, above, 2, d))

    def tokens_here():
        for plane in range(4):
            place = plane * 2 + 1 - y
            settle(normed.at[token_rows(place)], token_recv.at[place])

    def mix(j, span):
        columns = pl.ds(j * chunk, chunk)
        inputs = normed[span, :]
        gate_sum = jnp.dot(inputs, weights[0, :, columns], preferred_element_type=jnp.float32)
        upper_sum = jnp.dot(inputs, weights[1, :, columns], preferred_element_type=jnp.float32)
        hidden = (gate_sum / (1.0 + jnp.exp(-gate_sum)) * upper_sum).astype(jnp.bfloat16)
        return against(hidden, weights[2, :, columns])

    half_rows = 4 * rows

    def early(j, half):
        span = pl.ds(half * half_rows, half_rows)
        if j == 0:
            total[span, :] = mix(j, span)
        else:
            total[span, :] += mix(j, span)

    spread_tokens(0)
    relay(*near[3])
    relay(*near[8])
    issue(*near[0])
    relay(*near[1])
    spread_tokens(1)
    spread_tokens(2)
    relay(*near[0])
    relay_across(1, 1)
    issue(*far[2])
    relay_across(2, 2)
    relay(*far[7])
    relay_across(0, 1)
    relay_across(*far[3])
    relay(*near[5])
    relay(*far[10])
    issue(*far[9])
    relay(*far[2])
    relay_across(1, 2)
    issue(*far[6])
    relay_across(2, 1)
    relay_across(*far[5])
    spread_tokens(3)
    relay_across(0, 2)
    relay_across(*far[7])
    relay_across(*far[2])
    relay_across(2, 3)
    issue(*far[8])
    relay(*far[9])
    relay_across(*far[10])
    relay_across(*far[1])
    relay_across(0, 0)
    settle(weights.at[:, pl.ds(0, strip), pl.ds(0, units)], own_sem)
    chunk_done(0)
    relay(*far[6])
    relay_across(1, 0)
    tokens_here()
    relay(*far[8])
    issue(*far[11])
    early(0, 0)
    relay_across(1, 3)
    relay_across(*far[6])
    early(0, 1)
    chunk_done(1)
    relay(*far[11])
    early(1, 0)
    early(1, 1)
    relay_across(*far[9])
    relay_across(*far[8])
    relay_across(*far[11])
    chunk_done(2)

    upper_half = z // 2
    folded_z = z + upper_half * (3 - 2 * z)

    def plane_of(i):
        base = (3, 2, 1 - folded_z, folded_z)[i]
        return base + upper_half * (3 - 2 * base)

    front = pair_out.shape[2]
    early_lanes, late_lanes = pl.ds(0, front), pl.ds(front, width - front)

    def last(i):
        plane = plane_of(i)
        span = token_rows(plane * 2, 2)
        away = token_rows(plane * 2 + 1 - y)
        first = away if i == 0 else span
        total[first, :] += mix(CHUNKS - 1, first)
        pair_out[i] = total[away, early_lanes].astype(jnp.bfloat16)
        push(pair_out.at[i], pair_in.at[i], pair_send.at[i], pair_recv.at[i], in_plane(beside))
        if i == 0:
            rest = token_rows(plane * 2 + y)
            total[rest, :] += mix(CHUNKS - 1, rest)

    def column_sum(i):
        settle(pair_in.at[i], pair_recv.at[i])
        own = token_rows(plane_of(i) * 2 + y)
        total[own, early_lanes] += pair_in[i].astype(jnp.float32)
        return own

    def add_early(span, way, plane):
        settle(chain_in.at[way, plane], chain_recv.at[way, plane])
        total[span, early_lanes] += chain_in[way, plane].astype(jnp.float32)

    def add_late(span, way, plane):
        settle(late_in.at[way, plane], late_recv.at[way, plane])
        total[span, late_lanes] += late_in[way, plane].astype(jnp.float32)

    def onward(i, span, lanes_of, add, out, into, send_sem, recv_sem):
        plane = plane_of(i)

        def go(way, device, has_more):
            @pl.when(has_more)
            def _():
                add(span, way, plane)

            out[i] = total[span, lanes_of].astype(jnp.bfloat16)
            push(out.at[i], into.at[way, plane], send_sem.at[i], recv_sem.at[way, plane], device)

        pl.when(plane > z)(lambda: go(0, in_plane(p + 2), z > 0))
        pl.when(plane < z)(lambda: go(1, in_plane(p - 2), z < 3))

    def along(i):
        own = column_sum(i)
        onward(i, own, early_lanes, add_early, chain_out, chain_in, chain_send, chain_recv)

    def along_late(i):
        span = token_rows(plane_of(i) * 2, 2)
        onward(i, span, late_lanes, add_late, late_out, late_in, late_send, late_recv)

    def settle_late():
        span = token_rows(z * 2, 2)
        pl.when(z > 0)(lambda: add_late(span, 0, z))
        pl.when(z < 3)(lambda: add_late(span, 1, z))
        late_pair_out[...] = total[token_rows(beside), late_lanes].astype(jnp.bfloat16)
        push(late_pair_out, late_pair_in, late_pair_send, late_pair_recv, in_plane(beside))

    last(0)
    last(1)
    along_late(0)
    last(2)
    along_late(1)
    last(3)
    along_late(2)
    along(0)
    along(1)
    settle_late()
    along(2)
    own = column_sum(3)
    pl.when(z > 0)(lambda: add_early(own, 0, z))
    pl.when(z < 3)(lambda: add_early(own, 1, z))
    settle(late_pair_in, late_pair_recv)
    total[own, late_lanes] += late_pair_in[...].astype(jnp.float32)
    out_ref[...] = (own_attended[...].astype(jnp.float32) + total[own, :]).astype(jnp.bfloat16)

    for j in range(CHUNKS):
        settle(weights.at[:, pl.ds(0, 7 * strip), pl.ds(0, piece)], plane_send.at[j])
    settle(weights.at[:, pl.ds(0, 8 * strip), pl.ds(0, units)], across_send)
    settle(weights.at[:, :, pl.ds(0, units)], core_send)
    settle(share_out, share_send)
    tokens_sent()
    for i in range(4):
        settle(pair_out.at[i], pair_send.at[i])
    for i in range(3):
        settle(chain_out.at[i], chain_send.at[i])
        settle(late_out.at[i], late_send.at[i])
    settle(late_pair_out, late_pair_send)


def window(
    queries,
    cached_key_slots,
    cached_value_slots,
    new_token_keys,
    new_token_values,
    cache_len,
    placing,
    w_gate,
    w_up,
    w_down,
):
    tokens, width = queries.shape
    rows = tokens // 2
    bf16, f32 = jnp.bfloat16, jnp.float32
    vmem, dma = pltpu.VMEM, pltpu.SemaphoreType.DMA
    hidden_units = w_gate.shape[1] // 4
    late = width // 6
    scalars = pl.BlockSpec(memory_space=pltpu.SMEM)
    return pl.pallas_call(
        window_kernel,
        out_shape=jax.ShapeDtypeStruct((rows, width), bf16),
        in_specs=[scalars] * 2 + [pl.BlockSpec(memory_space=pl.ANY)] * 8,
        out_specs=pl.BlockSpec(memory_space=pltpu.VMEM),
        scratch_shapes=[
            vmem((3, width, hidden_units), bf16),
            vmem(cached_key_slots.shape, bf16),
            vmem(cached_value_slots.shape, bf16),
            vmem((tokens, width), bf16),
            vmem(new_token_keys.shape, bf16),
            vmem(new_token_values.shape, bf16),
            vmem((QUERY_HEADS, tokens, HEAD_SIZE), f32),
            vmem((QUERY_HEADS, tokens, 128), f32),
            vmem((QUERY_HEADS, tokens, 128), f32),
            vmem((QUERY_HEADS, rows, 2 * HEAD_SIZE), f32),
            vmem((QUERY_HEADS, rows, 2 * HEAD_SIZE), f32),
            vmem((rows, width), bf16),
            vmem((8 * rows, width), bf16),
            vmem((8 * rows, width), f32),
            vmem((4, rows, width - late), bf16),
            vmem((4, rows, width - late), bf16),
            vmem((3, rows, width - late), bf16),
            vmem((2, 4, rows, width - late), bf16),
            vmem((3, tokens, late), bf16),
            vmem((2, 4, tokens, late), bf16),
            vmem((rows, late), bf16),
            vmem((rows, late), bf16),
            dma((CHUNKS,)),
            dma((CHUNKS, 8)),
            dma,
            dma((CHUNKS, 8)),
            dma,
            dma((CHUNKS,)),
            dma,
            dma((3,)),
            dma((2, CACHE_PARTS)),
            dma,
            dma,
            dma((3, 7)),
            dma((8,)),
            dma((4,)),
            dma((4,)),
            dma((3,)),
            dma((2, 4)),
            dma((3,)),
            dma((2, 4)),
            dma,
            dma,
        ],
        compiler_params=pltpu.CompilerParams(
            collective_id=0, has_side_effects=True, vmem_limit_bytes=60 * 1024 * 1024
        ),
        name="window",
    )(
        cache_len,
        placing,
        queries,
        cached_key_slots,
        cached_value_slots,
        new_token_keys,
        new_token_values,
        w_gate,
        w_up,
        w_down.T,
    )


def body(
    queries,
    cached_key_slots,
    cached_value_slots,
    new_token_keys,
    new_token_values,
    cache_len,
    placing,
    w_gate,
    w_up,
    w_down,
):
    if lax.axis_size("req") != 16 or lax.axis_size("mlp") != 2:
        return wide_body(
            queries,
            cached_key_slots,
            cached_value_slots,
            new_token_keys,
            new_token_values,
            cache_len,
            placing,
            w_gate,
            w_up,
            w_down,
        )
    return window(
        queries[0],
        cached_key_slots[0],
        cached_value_slots[0],
        new_token_keys[0],
        new_token_values[0],
        cache_len,
        placing,
        w_gate,
        w_up,
        w_down,
    )[None]


def solution(mesh):
    in_specs = (
        P("req", None, None),
        P("req", "mlp", None),
        P("req", "mlp", None),
        P("req", "mlp", None),
        P("req", "mlp", None),
        P(),
        P(),
        P("req", "mlp"),
        P("req", "mlp"),
        P("mlp", "req"),
    )
    out_specs = P("req", "mlp", None)
    return jax.shard_map(body, mesh=mesh, in_specs=in_specs, out_specs=out_specs, check_vma=False)
```
